128 devices in a mesh: body: 8 (over z, core), blk: 16 (over y, x).
Axes of the slice: x: 4, y: 4, z: 4, core: 2. Of those that a mesh axis runs over, the one named last changes fastest.
Arguments:
- state: bfloat16 [1536, 320, 128], P(('body', 'blk')), may hold values from -6 to 6
- diag_tiles: bfloat16 [1536, 320, 320], P(('body', 'blk')), may hold values from -0.125 to 0.125
- nbr_tiles: bfloat16 [1536, 4, 320, 320], P(('body', 'blk')), may hold values from -0.125 to 0.125
- nbr_list: int32 [1536, 4], P(('body', 'blk')), may hold values from 0 to 11
- donor_tiles: bfloat16 [6144, 320, 320], P(('body', 'blk')), may hold values from -0.15625 to 0.15625
- donor_src: int32 [6144, 4], P(('body', 'blk')), may hold values from 0 to 11
- donor_slot: int32 [6144], P(('body', 'blk')), may hold values from 0 to 127, as said below
- donor_recv: int32 [6144], P(('body', 'blk')), may hold values from 0 to 11
- phase: int32 [2], replicated, may hold values from 0 to 3
Outputs:
- first: bfloat16 [1536, 320, 128], P(('body', 'blk'))
- second: bfloat16 [1536, 320, 128], P(('body', 'blk'))
The draws below stay inside these ranges and needn't reach their ends.
Inputs may be any that keep to these rules, and one draw needn't show every extreme that they name: `donor_slot`: the 48 donor tiles of one device have distinct slots, so at most 1 of them feed any one device.
All inputs are finite; a program needn't handle non-finite values.
Results may differ from the reference program's by a relative error of at most 0.0058.
Values may be sent and summed in bfloat16 or wider, within the bound.
No kernel may reach another device: no remote copies, remote signals or barrier semaphores. Data moves between devices by JAX's collectives and lax.ppermute only.
A program may use at most 192 MiB of HBM per device.

```python
import jax
import jax.numpy as jnp
from jax import lax

LINE = 320
KN = 4
PH = 4
NV = 128
NB = 12
ND = 48
PEERS = 128
CAP = 1
NBLK_ALL = 1536
DON_ALL = 6144
N_BODY = 8
N_BLK = 16


def draw_donor_slot(key, part):
    keys = jax.random.split(key, PEERS)

    def one_row(row_key):
        return jax.random.permutation(row_key, PEERS * CAP)[:ND]
    return jax.vmap(one_row)(keys).reshape(-1).astype(jnp.int32)


def set_ends(entries, rng, least, high):
    longest = entries.shape.index(max(entries.shape))
    spots = []
    for shift in (0, 1):
        where = [jax.random.randint(jax.random.fold_in(rng, axis), (), 0, length) for axis, length in enumerate(entries.shape)]
        where[longest] = (where[longest] + shift) % entries.shape[longest]
        spots.append(tuple(where))
    return entries.at[spots[0]].set(least).at[spots[1]].set(high)


def steps_of(stream_key, extent, cuts, low, top_value):
    gain, own = 1.0, jax.random.fold_in(stream_key, 6)
    for position, blocks in cuts:
        steps = jnp.exp(jax.random.uniform(jax.random.fold_in(own, position), (blocks,), jnp.float32, low / len(cuts), top_value / len(cuts)))
        gain = gain * jnp.repeat(steps, extent[position] // blocks).reshape([-1 if axis == position else 1 for axis in range(len(extent))])
    return gain


def bell_draw(own_key, shape, width, limit, cuts=(), held_as=jnp.bfloat16):
    result = jax.random.normal(own_key, shape, jnp.float32) * width
    if len(cuts) > 0:
        result = steps_of(own_key, shape, cuts, -0.22, 0.18) * result
    return jnp.clip(result, min=-limit, max=limit).astype(held_as)


def setup_inputs(seed: int = 0) -> dict:
    key_of = jax.random.split(jax.random.key(seed), 10)
    return {
        "state": bell_draw(key_of[0], (NBLK_ALL, LINE, NV), 1.0, 6.0, ((0, 128),)),
        "diag_tiles": bell_draw(key_of[1], (NBLK_ALL, LINE, LINE), (6 * LINE) ** -0.5, 0.125, ((0, 128),)),
        "nbr_tiles": bell_draw(key_of[2], (NBLK_ALL, KN, LINE, LINE), (6 * LINE) ** -0.5, 0.125, ((0, 128),)),
        "nbr_list": set_ends(jax.random.randint(key_of[3], (NBLK_ALL, KN), 0, NB), jax.random.fold_in(key_of[3], 1), 0, NB - 1).astype(jnp.int32),
        "donor_tiles": bell_draw(key_of[4], (DON_ALL, LINE, LINE), (4 * LINE) ** -0.5, 0.15625, ((0, 128),)),
        "donor_src": set_ends(jax.random.randint(key_of[5], (DON_ALL, PH), 0, NB), jax.random.fold_in(key_of[5], 1), 0, NB - 1).astype(jnp.int32),
        "donor_slot": draw_donor_slot(jax.random.fold_in(key_of[9], 71), 0),
        "donor_recv": set_ends(jax.random.randint(key_of[7], (DON_ALL,), 0, NB), jax.random.fold_in(key_of[7], 1), 0, NB - 1).astype(jnp.int32),
        "phase": jax.random.randint(key_of[8], (2,), 0, PH).astype(jnp.int32),
    }


def reference(state, diag_tiles, nbr_tiles, nbr_list, donor_tiles, donor_src, donor_slot, donor_recv, phase):
    peers = N_BODY * N_BLK
    diag_dev = diag_tiles.reshape(peers, NB, LINE, LINE)
    nbr_dev = nbr_tiles.reshape(peers, NB, KN, LINE, LINE)
    list_dev = nbr_list.reshape(peers, NB, KN)
    donor_dev = donor_tiles.reshape(peers, ND, LINE, LINE)
    target = ((donor_slot // CAP) * NB + donor_recv).astype(jnp.int32).reshape(peers, ND)

    def apply_op(vectors, column):
        vec_dev = vectors.reshape(peers, NB, LINE, NV)
        source = donor_src[:, column].reshape(peers, ND)

        def one_device(accum, pieces):
            diag_one, nbr_one, list_one, vec_one, donor_one, source_one, target_one = pieces
            vec_wide = vec_one.astype(jnp.float32)
            inner = jnp.einsum("bij,bjv->biv", diag_one.astype(jnp.float32), vec_wide)
            inner = inner + jnp.einsum("bkij,bkjv->biv", nbr_one.astype(jnp.float32), vec_wide[list_one])
            partial_value = jnp.einsum("eij,ejv->eiv", donor_one.astype(jnp.float32), vec_wide[source_one]).astype(jnp.bfloat16)
            accum = accum.at[target_one].add(partial_value.astype(jnp.float32))
            return accum, inner

        start = jnp.zeros((peers * NB, LINE, NV), jnp.float32)
        accum, inner = lax.scan(one_device, start, (diag_dev, nbr_dev, list_dev, vec_dev, donor_dev, source, target))
        return (inner.reshape(peers * NB, LINE, NV) + accum).astype(jnp.bfloat16)

    first = apply_op(state, phase[0])
    second = apply_op(first, phase[1])
    return first, second
```

```python
import functools

import jax
import jax.numpy as jnp
from jax import lax
from jax.experimental import pallas as pl
from jax.experimental.pallas import tpu as pltpu
from jax.sharding import PartitionSpec as P

AXES = ("body", "blk")
ANY = pl.BlockSpec(memory_space=pl.ANY)
VMEM = pl.BlockSpec(memory_space=pltpu.VMEM)
SMEM = pl.BlockSpec(memory_space=pltpu.SMEM)
LIMIT = 60 * 1024 * 1024
GROUP = 4


def dot(a, b):
    return jnp.dot(a, b, preferred_element_type=jnp.float32)


def product_kernel(source, slot, near, vectors, diag, nbr, donor, out, inner,
                   donor_buf, diag_buf, nbr_buf, made, donor_sem, diag_sem, nbr_sem, out_sem):
    count = donor.shape[0]
    blocks, fan = nbr.shape[0], nbr.shape[1]

    def donor_copy(g):
        part = pl.ds(g * GROUP, GROUP)
        return pltpu.make_async_copy(donor.at[part], donor_buf.at[part], donor_sem.at[g])

    def nbr_copy(b):
        return pltpu.make_async_copy(nbr.at[b], nbr_buf.at[b], nbr_sem.at[b])

    def out_copy(e):
        return pltpu.make_async_copy(made.at[e], out.at[slot[e]], out_sem.at[e])

    diag_copy = pltpu.make_async_copy(diag, diag_buf, diag_sem)
    for g in range(count // GROUP):
        donor_copy(g).start()
    diag_copy.start()
    for b in range(blocks):
        nbr_copy(b).start()

    @pl.loop(0, count // GROUP)
    def _(g):
        donor_copy(g).wait()
        for i in range(GROUP):
            e = g * GROUP + i
            made[e] = dot(donor_buf[e], vectors[source[e]]).astype(made.dtype)
            out_copy(e).start()

    diag_copy.wait()

    @pl.loop(0, blocks)
    def _(b):
        nbr_copy(b).wait()
        total = dot(diag_buf[b], vectors[b])
        for k in range(fan):
            total = total + dot(nbr_buf[b, k], vectors[near[b * fan + k]])
        inner[b] = total

    @pl.loop(0, count)
    def _(e):
        out_copy(e).wait()


def products(source, slot, near, vectors, diag, nbr, donor, slots):
    count = donor.shape[0]
    blocks, width, columns = vectors.shape
    return pl.pallas_call(
        product_kernel,
        out_shape=(
            jax.ShapeDtypeStruct((slots, width, columns), vectors.dtype),
            jax.ShapeDtypeStruct((blocks, width, columns), jnp.float32),
        ),
        in_specs=[SMEM, SMEM, SMEM, VMEM, ANY, ANY, ANY],
        out_specs=(ANY, VMEM),
        scratch_shapes=[
            pltpu.VMEM(donor.shape, donor.dtype),
            pltpu.VMEM(diag.shape, diag.dtype),
            pltpu.VMEM(nbr.shape, nbr.dtype),
            pltpu.VMEM((count, width, columns), vectors.dtype),
            pltpu.SemaphoreType.DMA((count // GROUP,)),
            pltpu.SemaphoreType.DMA,
            pltpu.SemaphoreType.DMA((blocks,)),
            pltpu.SemaphoreType.DMA((count,)),
        ],
        compiler_params=pltpu.CompilerParams(vmem_limit_bytes=LIMIT),
        name="products",
    )(source, slot, near, vectors, diag, nbr, donor)


def sum_kernel(target, inner, incoming, out, buf, total, sem):
    slots = incoming.shape[0]

    def copy(s):
        return pltpu.make_async_copy(incoming.at[s], buf.at[s], sem.at[s])

    @pl.loop(0, slots)
    def _(s):
        @pl.when(target[s] >= 0)
        def _():
            copy(s).start()

    total[...] = inner[...]

    @pl.loop(0, slots)
    def _(s):
        @pl.when(target[s] >= 0)
        def _():
            copy(s).wait()
            r = target[s]
            total[r] = total[r] + buf[s].astype(jnp.float32)

    out[...] = total[...].astype(out.dtype)


def summed(target, inner, incoming):
    return pl.pallas_call(
        sum_kernel,
        out_shape=jax.ShapeDtypeStruct(inner.shape, incoming.dtype),
        in_specs=[SMEM, VMEM, ANY],
        out_specs=VMEM,
        scratch_shapes=[
            pltpu.VMEM(incoming.shape, incoming.dtype),
            pltpu.VMEM(inner.shape, jnp.float32),
            pltpu.SemaphoreType.DMA((incoming.shape[0],)),
        ],
        compiler_params=pltpu.CompilerParams(vmem_limit_bytes=LIMIT),
        name="summed",
    )(target, inner, incoming)


def shards(state, diag, nbr, near, donor, donor_src, donor_slot, donor_recv, phase):
    slots = lax.axis_size("body") * lax.axis_size("blk")
    here = lax.axis_index("body") * lax.axis_size("blk") + lax.axis_index("blk")
    rows = lax.broadcasted_iota(jnp.int32, (slots, donor.shape[0]), 0)
    mine = jnp.max(jnp.where(rows == donor_slot[None, :], donor_recv[None, :], -1), axis=1)
    pattern = lax.all_gather(mine, AXES, axis=0, tiled=False)
    target = lax.dynamic_slice_in_dim(pattern, here, 1, axis=1)[:, 0]
    near = near.reshape(-1)
    columns = lax.broadcasted_iota(jnp.int32, donor_src.shape, 1)

    def apply_op(vectors, column):
        source = jnp.sum(jnp.where(columns == column, donor_src, 0), axis=1)
        outgoing, inner = products(source, donor_slot, near, vectors, diag, nbr, donor, slots)
        incoming = lax.all_to_all(outgoing, AXES, split_axis=0, concat_axis=0, tiled=True)
        return summed(target, inner, incoming)

    first = apply_op(state, phase[0])
    second = apply_op(first, phase[1])
    return first, second


def solution(mesh):
    split = P(AXES)
    return jax.shard_map(
        shards,
        mesh=mesh,
        in_specs=(split,) * 8 + (P(),),
        out_specs=(split, split),
        check_vma=False,
    )
```

```python
import functools

import jax
import jax.numpy as jnp
from jax import lax
from jax.experimental import pallas as pl
from jax.experimental.pallas import tpu as pltpu
from jax.sharding import PartitionSpec as P
import numpy as np

AXES = ("body", "blk")
ANY = pl.BlockSpec(memory_space=pl.ANY)
VMEM = pl.BlockSpec(memory_space=pltpu.VMEM)
SMEM = pl.BlockSpec(memory_space=pltpu.SMEM)
LIMIT = 60 * 1024 * 1024
GROUP = 4
SLOTS = 128
STREAMS, RING = 3, 4
REACH, CELL = 32, 8
FIRST, SECOND = 23, 25
ROWS = ((0, 112), (112, 112), (224, 96))
ORDERS = (("z", "y", "x"), ("y", "x", "z"), ("x", "z", "y"))


def dot(a, b):
    return jnp.dot(a, b, preferred_element_type=jnp.float32)


def product_kernel(source, slot, near, vectors, diag, nbr, donor, out, inner,
                   donor_buf, diag_buf, nbr_buf, made, donor_sem, diag_sem, nbr_sem, out_sem):
    count = donor.shape[0]
    blocks, fan = nbr.shape[0], nbr.shape[1]

    def donor_copy(g):
        part = pl.ds(g * GROUP, GROUP)
        return pltpu.make_async_copy(donor.at[part], donor_buf.at[part], donor_sem.at[g])

    def nbr_copy(b):
        return pltpu.make_async_copy(nbr.at[b], nbr_buf.at[b], nbr_sem.at[b])

    def out_copy(e):
        return pltpu.make_async_copy(made.at[e], out.at[slot[e]], out_sem.at[e])

    diag_copy = pltpu.make_async_copy(diag, diag_buf, diag_sem)
    for g in range(count // GROUP):
        donor_copy(g).start()
    diag_copy.start()
    for b in range(blocks):
        nbr_copy(b).start()

    @pl.loop(0, count // GROUP)
    def _(g):
        donor_copy(g).wait()
        for i in range(GROUP):
            e = g * GROUP + i
            made[e] = dot(donor_buf[e], vectors[source[e]]).astype(made.dtype)
            out_copy(e).start()

    diag_copy.wait()

    @pl.loop(0, blocks)
    def _(b):
        nbr_copy(b).wait()
        total = dot(diag_buf[b], vectors[b])
        for k in range(fan):
            total = total + dot(nbr_buf[b, k], vectors[near[b * fan + k]])
        inner[b] = total

    @pl.loop(0, count)
    def _(e):
        out_copy(e).wait()


def products(source, slot, near, vectors, diag, nbr, donor, slots):
    count = donor.shape[0]
    blocks, width, columns = vectors.shape
    return pl.pallas_call(
        product_kernel,
        out_shape=(
            jax.ShapeDtypeStruct((slots, width, columns), vectors.dtype),
            jax.ShapeDtypeStruct((blocks, width, columns), jnp.float32),
        ),
        in_specs=[SMEM, SMEM, SMEM, VMEM, ANY, ANY, ANY],
        out_specs=(ANY, VMEM),
        scratch_shapes=[
            pltpu.VMEM(donor.shape, donor.dtype),
            pltpu.VMEM(diag.shape, diag.dtype),
            pltpu.VMEM(nbr.shape, nbr.dtype),
            pltpu.VMEM((count, width, columns), vectors.dtype),
            pltpu.SemaphoreType.DMA((count // GROUP,)),
            pltpu.SemaphoreType.DMA,
            pltpu.SemaphoreType.DMA((blocks,)),
            pltpu.SemaphoreType.DMA((count,)),
        ],
        compiler_params=pltpu.CompilerParams(vmem_limit_bytes=LIMIT),
        name="products",
    )(source, slot, near, vectors, diag, nbr, donor)


def sum_kernel(target, inner, incoming, out, buf, total, sem):
    slots = incoming.shape[0]

    def copy(s):
        return pltpu.make_async_copy(incoming.at[s], buf.at[s], sem.at[s])

    @pl.loop(0, slots)
    def _(s):
        @pl.when(target[s] >= 0)
        def _():
            copy(s).start()

    total[...] = inner[...]

    @pl.loop(0, slots)
    def _(s):
        @pl.when(target[s] >= 0)
        def _():
            copy(s).wait()
            r = target[s]
            total[r] = total[r] + buf[s].astype(jnp.float32)

    out[...] = total[...].astype(out.dtype)


def summed(target, inner, incoming):
    return pl.pallas_call(
        sum_kernel,
        out_shape=jax.ShapeDtypeStruct(inner.shape, incoming.dtype),
        in_specs=[SMEM, VMEM, ANY],
        out_specs=VMEM,
        scratch_shapes=[
            pltpu.VMEM(incoming.shape, incoming.dtype),
            pltpu.VMEM(inner.shape, jnp.float32),
            pltpu.SemaphoreType.DMA((incoming.shape[0],)),
        ],
        compiler_params=pltpu.CompilerParams(vmem_limit_bytes=LIMIT),
        name="summed",
    )(target, inner, incoming)

def inner_kernel(near, vectors, diag, nbr, inner, diag_buf, nbr_buf, diag_sem, nbr_sem):
    blocks, fan = nbr.shape[0], nbr.shape[1]

    def nbr_copy(b):
        return pltpu.make_async_copy(nbr.at[b], nbr_buf.at[b], nbr_sem.at[b])

    diag_copy = pltpu.make_async_copy(diag, diag_buf, diag_sem)
    diag_copy.start()
    for b in range(blocks):
        nbr_copy(b).start()
    diag_copy.wait()

    @pl.loop(0, blocks)
    def _(b):
        nbr_copy(b).wait()
        total = dot(diag_buf[b], vectors[b])
        for k in range(fan):
            total = total + dot(nbr_buf[b, k], vectors[near[b * fan + k]])
        inner[b] = total


def interior(near, vectors, diag, nbr):
    blocks, width, columns = vectors.shape
    return pl.pallas_call(
        inner_kernel,
        out_shape=jax.ShapeDtypeStruct((blocks, width, columns), jnp.float32),
        in_specs=[SMEM, VMEM, ANY, ANY],
        out_specs=VMEM,
        scratch_shapes=[
            pltpu.VMEM(diag.shape, diag.dtype),
            pltpu.VMEM(nbr.shape, nbr.dtype),
            pltpu.SemaphoreType.DMA,
            pltpu.SemaphoreType.DMA((blocks,)),
        ],
        compiler_params=pltpu.CompilerParams(vmem_limit_bytes=LIMIT),
        cost_estimate=pl.CostEstimate(flops=4 * 10**9, bytes_accessed=2 * 10**7, transcendentals=0),
        name="interior",
    )(near, vectors, diag, nbr)


def donate_kernel(source, chosen, vectors, donor, *refs):
    outs, refs = refs[:STREAMS * RING], refs[STREAMS * RING:]
    packs, refs = refs[:STREAMS * RING], refs[STREAMS * RING:]
    donor_buf, made, donor_sem, out_sem = refs
    count = donor.shape[0]

    def donor_copy(g):
        part = pl.ds(g * GROUP, GROUP)
        return pltpu.make_async_copy(donor.at[part], donor_buf.at[part], donor_sem.at[g])

    for g in range(count // GROUP):
        donor_copy(g).start()

    @pl.loop(0, count // GROUP)
    def _(g):
        donor_copy(g).wait()
        for i in range(GROUP):
            e = g * GROUP + i
            made[e] = dot(donor_buf[e], vectors[source[e]]).astype(made.dtype)

    copies = []
    for s, (start, rows) in enumerate(ROWS):
        for k in range(RING):
            pack = packs[s * RING + k]
            base = (s * RING + k) * REACH

            def step(j, held, pack=pack, base=base, start=start, rows=rows):
                e = chosen[base + j]
                pack[jnp.minimum(held, FIRST)] = made[jnp.maximum(e, 0), pl.ds(start, rows)]
                return held + (e >= 0).astype(jnp.int32)

            lax.fori_loop(0, REACH, step, jnp.int32(0), unroll=8)
            copy = pltpu.make_async_copy(
                pack.at[pl.ds(0, FIRST)], outs[s * RING + k], out_sem.at[s * RING + k]
            )
            copy.start()
            copies.append(copy)
    for copy in copies:
        copy.wait()


def donate(source, chosen, vectors, donor):
    count = donor.shape[0]
    width, columns = vectors.shape[1:]
    shapes = [(rows, columns) for _, rows in ROWS for _ in range(RING)]
    return pl.pallas_call(
        donate_kernel,
        out_shape=tuple(jax.ShapeDtypeStruct((FIRST,) + s, vectors.dtype) for s in shapes),
        in_specs=[SMEM, SMEM, VMEM, ANY],
        out_specs=(ANY,) * len(shapes),
        scratch_shapes=[pltpu.VMEM((FIRST + 1,) + s, vectors.dtype) for s in shapes]
        + [
            pltpu.VMEM(donor.shape, donor.dtype),
            pltpu.VMEM((count, width, columns), vectors.dtype),
            pltpu.SemaphoreType.DMA((count // GROUP,)),
            pltpu.SemaphoreType.DMA((len(shapes),)),
        ],
        compiler_params=pltpu.CompilerParams(vmem_limit_bytes=LIMIT),
        name="donate",
    )(source, chosen, vectors, donor)


def relay_kernel(table, *refs):
    ins, outs, packs, sem = refs[:RING], refs[RING:2 * RING], refs[2 * RING:3 * RING], refs[-1]
    held = [jnp.int32(0)] * RING
    for i in range(RING):
        taken = jnp.int32(0)
        for k in range(RING):
            base = (i * RING + k) * CELL
            for j in range(CELL):
                real = (table[base + j] >= 0).astype(jnp.int32)
                packs[k][jnp.minimum(held[k], SECOND)] = ins[i][jnp.minimum(taken, FIRST - 1)]
                held[k] = held[k] + real
                taken = taken + real
    copies = []
    for k in range(RING):
        copy = pltpu.make_async_copy(packs[k].at[pl.ds(0, SECOND)], outs[k], sem.at[k])
        copy.start()
        copies.append(copy)
    for copy in copies:
        copy.wait()


def relay(table, ins):
    shape, kind = ins[0].shape[1:], ins[0].dtype
    return pl.pallas_call(
        relay_kernel,
        out_shape=(jax.ShapeDtypeStruct((SECOND,) + shape, kind),) * RING,
        in_specs=[SMEM] + [VMEM] * RING,
        out_specs=(ANY,) * RING,
        scratch_shapes=[pltpu.VMEM((SECOND + 1,) + shape, kind)] * RING
        + [pltpu.SemaphoreType.DMA((RING,))],
        compiler_params=pltpu.CompilerParams(vmem_limit_bytes=LIMIT),
        cost_estimate=pl.CostEstimate(flops=10**6, bytes_accessed=6 * 10**6, transcendentals=0),
        name="relay",
    )(table, *ins)


def gather_kernel(table, *refs):
    ins, (own, flip, total) = refs[:RING], refs[RING:]
    blocks = own.shape[0] // RING
    total[...] = jnp.zeros_like(total)
    for i in range(RING):

        def step(q, taken, i=i):
            for f in range(2):
                for k in range(RING):
                    r = table[((i * RING + q) * 2 + f) * RING + k]
                    real = r >= 0
                    slot = jnp.minimum(taken, SECOND - 1)
                    cell = (f * RING + k) * blocks + r

                    @pl.when(real)
                    def _(slot=slot, cell=cell):
                        total[cell] = total[cell] + ins[i][slot].astype(jnp.float32)

                    taken = taken + real.astype(jnp.int32)
            return taken

        lax.fori_loop(0, RING, step, jnp.int32(0))
    own[...] = total[pl.ds(0, RING * blocks)]
    flip[...] = total[pl.ds(RING * blocks, RING * blocks)].astype(flip.dtype)


def gathered(table, ins, blocks):
    shape, kind = ins[0].shape[1:], ins[0].dtype
    return pl.pallas_call(
        gather_kernel,
        out_shape=(
            jax.ShapeDtypeStruct((RING * blocks,) + shape, jnp.float32),
            jax.ShapeDtypeStruct((RING * blocks,) + shape, kind),
        ),
        in_specs=[SMEM] + [VMEM] * RING,
        out_specs=(VMEM, VMEM),
        scratch_shapes=[pltpu.VMEM((2 * RING * blocks,) + shape, jnp.float32)],
        compiler_params=pltpu.CompilerParams(vmem_limit_bytes=LIMIT),
        cost_estimate=pl.CostEstimate(flops=10**6, bytes_accessed=6 * 10**6, transcendentals=0),
        name="gathered",
    )(table, *ins)


def join_kernel(own, flip, *outs):
    blocks = outs[0].shape[0]
    for k in range(RING):
        part = pl.ds(k * blocks, blocks)
        outs[k][...] = (own[part] + flip[part].astype(jnp.float32)).astype(outs[k].dtype)


def joined(own, flip):
    blocks = own.shape[0] // RING
    return pl.pallas_call(
        join_kernel,
        out_shape=(jax.ShapeDtypeStruct((blocks,) + own.shape[1:], flip.dtype),) * RING,
        in_specs=[VMEM, VMEM],
        out_specs=(VMEM,) * RING,
        compiler_params=pltpu.CompilerParams(vmem_limit_bytes=LIMIT),
        cost_estimate=pl.CostEstimate(flops=10**6, bytes_accessed=5 * 10**6, transcendentals=0),
        name="joined",
    )(own, flip)


def final_kernel(inner, *refs):
    parts, out = refs[:-1], refs[-1]
    for s, (start, rows) in enumerate(ROWS):
        part = pl.ds(start, rows)
        total = inner[:, part]
        for k in range(RING):
            total = total + parts[s * RING + k][...].astype(jnp.float32)
        out[:, part] = total.astype(out.dtype)


def final(inner, parts):
    return pl.pallas_call(
        final_kernel,
        out_shape=jax.ShapeDtypeStruct(inner.shape, parts[0].dtype),
        in_specs=[VMEM] * (1 + len(parts)),
        out_specs=VMEM,
        compiler_params=pltpu.CompilerParams(vmem_limit_bytes=LIMIT),
        name="final",
    )(inner, *parts)


def place(index):
    return {"z": index // 32, "core": index // 16 % 2, "y": index // 4 % 4, "x": index % 4}


def number(at):
    return ((at["z"] * 2 + at["core"]) * 4 + at["y"]) * 4 + at["x"]


def shift(value, axis, step):
    if axis in ("z", "core"):
        name, size = "body", 8
        move = (lambda i: (i + 2 * step) % 8) if axis == "z" else (lambda i: i ^ 1)
    else:
        name, size = "blk", 16
        if axis == "y":
            move = lambda i: (i + 4 * step) % 16
        else:
            move = lambda i: i // 4 * 4 + (i + step) % 4
    return lax.ppermute(value, name, [(i, move(i)) for i in range(size)])


def offsets(order):
    grid = np.meshgrid(*[np.arange(2 if n == "f" else 4) for n in order], indexing="ij")
    return {n: g.reshape(-1) for n, g in zip(order, grid)}


def tables(here, mine, pattern):
    me = place(here)
    wanted, senders, takers = [], [], []
    for one, two, three in ORDERS:
        o = offsets(("1", "2", "f", "3"))
        at = dict(me)
        at[one], at[two], at[three] = ((me[n] + o[k]) % 4 for n, k in ((one, "1"), (two, "2"), (three, "3")))
        at["core"] = me["core"] ^ o["f"]
        wanted.append(number(at))
    for stage in (2, 3):
        for one, two, three in ORDERS:
            o = offsets(("1", "2", "f", "3") if stage == 2 else ("2", "1", "f", "3"))
            sender, taker = dict(me), dict(me)
            sender[one] = (me[one] - o["1"]) % 4
            if stage == 3:
                sender[two] = (me[two] - o["2"]) % 4
            else:
                taker[two] = (me[two] + o["2"]) % 4
            taker["core"] = me["core"] ^ o["f"]
            taker[three] = (me[three] + o["3"]) % 4
            senders.append(number(sender) + jnp.zeros((SLOTS,), jnp.int32))
            takers.append(number(taker) + jnp.zeros((SLOTS,), jnp.int32))
    wanted = jnp.concatenate(wanted)
    senders, takers = jnp.concatenate(senders), jnp.concatenate(takers)
    ids = jnp.arange(SLOTS, dtype=jnp.int32)
    chosen = jnp.max(jnp.where(ids[:, None] == wanted[None, :], mine[:, None], -1), axis=0)
    picked = dot((senders[:, None] == ids[None, :]).astype(jnp.bfloat16), (pattern + 1).astype(jnp.bfloat16))
    picked = jnp.sum(jnp.where(takers[:, None] == ids[None, :], picked, 0.0), axis=1).astype(jnp.int32) - 1
    second, third = picked.reshape(2, STREAMS, SLOTS)
    return chosen, second, third


def overflows(pattern):
    real = (pattern >= 0).astype(jnp.bfloat16)
    at = place(np.arange(SLOTS))
    firsts, lefts, rights = [], [], []
    for one, two, three in ORDERS:
        firsts.append(np.arange(4)[None, :] == at[one][:, None])
        lefts.append(np.arange(32)[:, None] == ((at["core"] * 4 + at[two]) * 4 + at[three])[None, :])
        rights.append(np.arange(16)[None, :] == (at[one] * 4 + at[two])[:, None])
    firsts = jnp.asarray(np.concatenate(firsts, 1), jnp.bfloat16)
    lefts = jnp.asarray(np.concatenate(lefts, 0), jnp.bfloat16)
    rights = jnp.asarray(np.concatenate(rights, 1), jnp.bfloat16)
    same = (np.arange(STREAMS * 32) // 32)[:, None] == (np.arange(STREAMS * 16) // 16)[None, :]
    one = jnp.max(dot(real, firsts))
    two = jnp.max(jnp.where(same, dot(dot(lefts, real).astype(jnp.bfloat16), rights), 0.0))
    return (one > FIRST) | (two > SECOND)


def shards(state, diag, nbr, near, donor, donor_src, donor_slot, donor_recv, phase):
    here = lax.axis_index("body") * lax.axis_size("blk") + lax.axis_index("blk")
    rows = lax.broadcasted_iota(jnp.int32, (SLOTS, donor.shape[0]), 0)
    hit = rows == donor_slot[None, :]
    mine = jnp.max(jnp.where(hit, lax.broadcasted_iota(jnp.int32, hit.shape, 1), -1), axis=1)
    recv = jnp.max(jnp.where(hit, donor_recv[None, :], -1), axis=1)
    pattern = lax.all_gather(recv, AXES, axis=0, tiled=False)
    chosen, second, third = tables(here, mine, pattern)
    near = near.reshape(-1)
    columns = lax.broadcasted_iota(jnp.int32, donor_src.shape, 1)
    sources = [jnp.sum(jnp.where(columns == phase[i], donor_src, 0), axis=1) for i in range(2)]
    state, chosen = lax.optimization_barrier((state, chosen, pattern))[:2]

    def dense(vectors, source):
        target = lax.dynamic_slice_in_dim(pattern, here, 1, axis=1)[:, 0]
        outgoing, inner = products(source, donor_slot, near, vectors, diag, nbr, donor, SLOTS)
        incoming = lax.all_to_all(outgoing, AXES, split_axis=0, concat_axis=0, tiled=True)
        return summed(target, inner, incoming)

    def staged(vectors, source):
        sent = donate(source, chosen, vectors, donor)
        inner = interior(near, vectors, diag, nbr)
        parts = []
        flight = [
            [sent[s * RING]] + [shift(sent[s * RING + k], ORDERS[s][0], k) for k in range(1, RING)]
            for s in range(STREAMS)
        ]
        passed = [relay(second[s], flight[s]) for s in range(STREAMS)]
        flight = [
            [passed[s][0]] + [shift(passed[s][k], ORDERS[s][1], k) for k in range(1, RING)]
            for s in range(STREAMS)
        ]
        for s in range(STREAMS):
            own, flip = gathered(third[s], flight[s], vectors.shape[0])
            ready = joined(own, shift(flip, "core", 1))
            parts += [ready[0]] + [shift(ready[k], ORDERS[s][2], k) for k in range(1, RING)]
        return final(inner, parts)

    def all_dense():
        first = dense(state, sources[0])
        return first, dense(first, sources[1])

    first = staged(state, sources[0])
    second_out = staged(first, sources[1])
    return lax.cond(overflows(pattern), all_dense, lambda: (first, second_out))


def solution(mesh):
    split = P(AXES)
    return jax.shard_map(
        shards,
        mesh=mesh,
        in_specs=(split,) * 8 + (P(),),
        out_specs=(split, split),
        check_vma=False,
    )
```

```python
import functools

import jax
import jax.numpy as jnp
from jax import lax
from jax.experimental import pallas as pl
from jax.experimental.pallas import tpu as pltpu
from jax.sharding import PartitionSpec as P
import numpy as np

AXES = ("body", "blk")
ANY = pl.BlockSpec(memory_space=pl.ANY)
VMEM = pl.BlockSpec(memory_space=pltpu.VMEM)
SMEM = pl.BlockSpec(memory_space=pltpu.SMEM)
LIMIT = 60 * 1024 * 1024


def near_core(shape, kind):
    return pltpu.VMEM(shape, kind)


def pinned(values):
    return [pltpu.with_memory_space_constraint(v, pltpu.VMEM) for v in values]


GROUP = 4
SLOTS = 128
STREAMS, RING = 3, 4
REACH, CELL = 32, 8
FIRST, SECOND = 23, 25
ROWS = ((0, 112), (112, 112), (224, 96))
ORDERS = (("z", "y", "x"), ("y", "x", "z"), ("x", "z", "y"))


def dot(a, b):
    return jnp.dot(a, b, preferred_element_type=jnp.float32)


def product_kernel(source, slot, near, vectors, diag, nbr, donor, out, inner,
                   donor_buf, diag_buf, nbr_buf, made, donor_sem, diag_sem, nbr_sem, out_sem):
    count = donor.shape[0]
    blocks, fan = nbr.shape[0], nbr.shape[1]

    def donor_copy(g):
        part = pl.ds(g * GROUP, GROUP)
        return pltpu.make_async_copy(donor.at[part], donor_buf.at[part], donor_sem.at[g])

    def nbr_copy(b):
        return pltpu.make_async_copy(nbr.at[b], nbr_buf.at[b], nbr_sem.at[b])

    def out_copy(e):
        return pltpu.make_async_copy(made.at[e], out.at[slot[e]], out_sem.at[e])

    diag_copy = pltpu.make_async_copy(diag, diag_buf, diag_sem)
    for g in range(count // GROUP):
        donor_copy(g).start()
    diag_copy.start()
    for b in range(blocks):
        nbr_copy(b).start()

    @pl.loop(0, count // GROUP)
    def _(g):
        donor_copy(g).wait()
        for i in range(GROUP):
            e = g * GROUP + i
            made[e] = dot(donor_buf[e], vectors[source[e]]).astype(made.dtype)
            out_copy(e).start()

    diag_copy.wait()

    @pl.loop(0, blocks)
    def _(b):
        nbr_copy(b).wait()
        total = dot(diag_buf[b], vectors[b])
        for k in range(fan):
            total = total + dot(nbr_buf[b, k], vectors[near[b * fan + k]])
        inner[b] = total

    @pl.loop(0, count)
    def _(e):
        out_copy(e).wait()


def products(source, slot, near, vectors, diag, nbr, donor, slots):
    count = donor.shape[0]
    blocks, width, columns = vectors.shape
    return pl.pallas_call(
        product_kernel,
        out_shape=(
            jax.ShapeDtypeStruct((slots, width, columns), vectors.dtype),
            jax.ShapeDtypeStruct((blocks, width, columns), jnp.float32),
        ),
        in_specs=[SMEM, SMEM, SMEM, VMEM, ANY, ANY, ANY],
        out_specs=(ANY, VMEM),
        scratch_shapes=[
            pltpu.VMEM(donor.shape, donor.dtype),
            pltpu.VMEM(diag.shape, diag.dtype),
            pltpu.VMEM(nbr.shape, nbr.dtype),
            pltpu.VMEM((count, width, columns), vectors.dtype),
            pltpu.SemaphoreType.DMA((count // GROUP,)),
            pltpu.SemaphoreType.DMA,
            pltpu.SemaphoreType.DMA((blocks,)),
            pltpu.SemaphoreType.DMA((count,)),
        ],
        compiler_params=pltpu.CompilerParams(vmem_limit_bytes=LIMIT),
        name="products",
    )(source, slot, near, vectors, diag, nbr, donor)


def sum_kernel(target, inner, incoming, out, buf, total, sem):
    slots = incoming.shape[0]

    def copy(s):
        return pltpu.make_async_copy(incoming.at[s], buf.at[s], sem.at[s])

    @pl.loop(0, slots)
    def _(s):
        @pl.when(target[s] >= 0)
        def _():
            copy(s).start()

    total[...] = inner[...]

    @pl.loop(0, slots)
    def _(s):
        @pl.when(target[s] >= 0)
        def _():
            copy(s).wait()
            r = target[s]
            total[r] = total[r] + buf[s].astype(jnp.float32)

    out[...] = total[...].astype(out.dtype)


def summed(target, inner, incoming):
    return pl.pallas_call(
        sum_kernel,
        out_shape=jax.ShapeDtypeStruct(inner.shape, incoming.dtype),
        in_specs=[SMEM, VMEM, ANY],
        out_specs=VMEM,
        scratch_shapes=[
            pltpu.VMEM(incoming.shape, incoming.dtype),
            pltpu.VMEM(inner.shape, jnp.float32),
            pltpu.SemaphoreType.DMA((incoming.shape[0],)),
        ],
        compiler_params=pltpu.CompilerParams(vmem_limit_bytes=LIMIT),
        name="summed",
    )(target, inner, incoming)

def inner_kernel(near, vectors, diag, nbr, inner, diag_buf, nbr_buf, diag_sem, nbr_sem):
    blocks, fan = nbr.shape[0], nbr.shape[1]

    def nbr_copy(b):
        return pltpu.make_async_copy(nbr.at[b], nbr_buf.at[b], nbr_sem.at[b])

    diag_copy = pltpu.make_async_copy(diag, diag_buf, diag_sem)
    diag_copy.start()
    for b in range(blocks):
        nbr_copy(b).start()
    diag_copy.wait()

    @pl.loop(0, blocks)
    def _(b):
        nbr_copy(b).wait()
        total = dot(diag_buf[b], vectors[b])
        for k in range(fan):
            total = total + dot(nbr_buf[b, k], vectors[near[b * fan + k]])
        inner[b] = total


def interior(near, vectors, diag, nbr):
    blocks, width, columns = vectors.shape
    return pl.pallas_call(
        inner_kernel,
        out_shape=near_core((blocks, width, columns), jnp.float32),
        in_specs=[SMEM, VMEM, ANY, ANY],
        out_specs=VMEM,
        scratch_shapes=[
            pltpu.VMEM(diag.shape, diag.dtype),
            pltpu.VMEM(nbr.shape, nbr.dtype),
            pltpu.SemaphoreType.DMA,
            pltpu.SemaphoreType.DMA((blocks,)),
        ],
        compiler_params=pltpu.CompilerParams(vmem_limit_bytes=18 * 2**20),
        cost_estimate=pl.CostEstimate(flops=4 * 10**9, bytes_accessed=2 * 10**7, transcendentals=0),
        name="interior",
    )(near, vectors, diag, nbr)


def donate_kernel(source, chosen, vectors, donor, *refs):
    outs, refs = refs[:STREAMS * RING], refs[STREAMS * RING:]
    donor_buf, made, donor_sem = refs
    count = donor.shape[0]

    def donor_copy(g):
        part = pl.ds(g * GROUP, GROUP)
        return pltpu.make_async_copy(donor.at[part], donor_buf.at[part], donor_sem.at[g])

    for g in range(count // GROUP):
        donor_copy(g).start()

    @pl.loop(0, count // GROUP)
    def _(g):
        donor_copy(g).wait()
        for i in range(GROUP):
            e = g * GROUP + i
            made[e] = dot(donor_buf[e], vectors[source[e]]).astype(made.dtype)

    for s, (start, rows) in enumerate(ROWS):
        for k in range(RING):
            out = outs[s * RING + k]
            base = (s * RING + k) * REACH

            def step(j, held, out=out, base=base, start=start, rows=rows):
                e = chosen[base + j]

                @pl.when((e >= 0) & (held < FIRST))
                def _():
                    out[held] = made[e, pl.ds(start, rows)]

                return held + (e >= 0).astype(jnp.int32)

            lax.fori_loop(0, REACH, step, jnp.int32(0), unroll=4)


def donate(source, chosen, vectors, donor):
    count = donor.shape[0]
    width, columns = vectors.shape[1:]
    shapes = [(rows, columns) for _, rows in ROWS for _ in range(RING)]
    return pl.pallas_call(
        donate_kernel,
        out_shape=tuple(near_core((FIRST,) + s, vectors.dtype) for s in shapes),
        in_specs=[SMEM, SMEM, VMEM, ANY],
        out_specs=(VMEM,) * len(shapes),
        scratch_shapes=[
            pltpu.VMEM(donor.shape, donor.dtype),
            pltpu.VMEM((count, width, columns), vectors.dtype),
            pltpu.SemaphoreType.DMA((count // GROUP,)),
        ],
        compiler_params=pltpu.CompilerParams(vmem_limit_bytes=20 * 2**20),
        name="donate",
    )(source, chosen, vectors, donor)


def relay_kernel(table, *refs):
    ins, outs = refs[:RING], refs[RING:]
    held = [jnp.int32(0)] * RING
    for i in range(RING):
        taken = jnp.int32(0)
        for k in range(RING):

            def step(j, both, i=i, k=k):
                into, out_of = both
                real = table[(i * RING + k) * CELL + j] >= 0

                @pl.when(real & (into < SECOND) & (out_of < FIRST))
                def _():
                    outs[k][into] = ins[i][out_of]

                one = real.astype(jnp.int32)
                return into + one, out_of + one

            held[k], taken = lax.fori_loop(0, CELL, step, (held[k], taken), unroll=4)


def relay(table, ins):
    shape, kind = ins[0].shape[1:], ins[0].dtype
    return pl.pallas_call(
        relay_kernel,
        out_shape=(near_core((SECOND,) + shape, kind),) * RING,
        in_specs=[SMEM] + [VMEM] * RING,
        out_specs=(VMEM,) * RING,
        compiler_params=pltpu.CompilerParams(vmem_limit_bytes=2**20),
        cost_estimate=pl.CostEstimate(flops=10**6, bytes_accessed=6 * 10**6, transcendentals=0),
        name="relay",
    )(table, *pinned(ins))


def gather_kernel(table, *refs):
    ins, (own, flip, total) = refs[:RING], refs[RING:]
    blocks = own.shape[0] // RING

    @pl.loop(0, RING * blocks)
    def _(cell):
        own[cell] = jnp.zeros(own.shape[1:], own.dtype)
        total[cell] = jnp.zeros(own.shape[1:], own.dtype)

    for i in range(RING):

        def step(q, taken, i=i):
            for f, sums in ((0, own), (1, total)):
                for k in range(RING):
                    r = table[((i * RING + q) * 2 + f) * RING + k]
                    real = r >= 0

                    @pl.when(real & (taken < SECOND))
                    def _(taken=taken, cell=k * blocks + r, sums=sums):
                        sums[cell] = sums[cell] + ins[i][taken].astype(jnp.float32)

                    taken = taken + real.astype(jnp.int32)
            return taken

        lax.fori_loop(0, RING, step, jnp.int32(0))

    @pl.loop(0, RING * blocks, unroll=2)
    def _(cell):
        flip[cell] = total[cell].astype(flip.dtype)


def gathered(table, ins, blocks):
    shape, kind = ins[0].shape[1:], ins[0].dtype
    return pl.pallas_call(
        gather_kernel,
        out_shape=(
            near_core((RING * blocks,) + shape, jnp.float32),
            near_core((RING * blocks,) + shape, kind),
        ),
        in_specs=[SMEM] + [VMEM] * RING,
        out_specs=(VMEM, VMEM),
        scratch_shapes=[pltpu.VMEM((RING * blocks,) + shape, jnp.float32)],
        compiler_params=pltpu.CompilerParams(vmem_limit_bytes=5 * 2**20),
        cost_estimate=pl.CostEstimate(flops=10**6, bytes_accessed=6 * 10**6, transcendentals=0),
        name="gathered",
    )(table, *pinned(ins))


def join_kernel(own, flip, *outs):
    blocks = outs[0].shape[0]

    @pl.loop(0, blocks)
    def _(b):
        for k in range(RING):
            both = own[k * blocks + b] + flip[k * blocks + b].astype(jnp.float32)
            outs[k][b] = both.astype(outs[k].dtype)


def joined(own, flip):
    blocks = own.shape[0] // RING
    return pl.pallas_call(
        join_kernel,
        out_shape=(near_core((blocks,) + own.shape[1:], flip.dtype),) * RING,
        in_specs=[VMEM, VMEM],
        out_specs=(VMEM,) * RING,
        compiler_params=pltpu.CompilerParams(vmem_limit_bytes=2**20),
        cost_estimate=pl.CostEstimate(flops=10**6, bytes_accessed=5 * 10**6, transcendentals=0),
        name="joined",
    )(*pinned((own, flip)))


def final_kernel(inner, *refs):
    parts, out = refs[:-1], refs[-1]

    @pl.loop(0, out.shape[0])
    def _(b):
        for s, (start, rows) in enumerate(ROWS):
            part = pl.ds(start, rows)
            total = inner[b, part]
            for k in range(RING):
                total = total + parts[s * RING + k][b].astype(jnp.float32)
            out[b, part] = total.astype(out.dtype)


def final(inner, parts):
    return pl.pallas_call(
        final_kernel,
        out_shape=jax.ShapeDtypeStruct(inner.shape, parts[0].dtype),
        in_specs=[VMEM] * (1 + len(parts)),
        out_specs=VMEM,
        compiler_params=pltpu.CompilerParams(vmem_limit_bytes=4 * 2**20),
        name="final",
    )(*pinned((inner, *parts)))


def place(index):
    return {"z": index // 32, "core": index // 16 % 2, "y": index // 4 % 4, "x": index % 4}


def number(at):
    return ((at["z"] * 2 + at["core"]) * 4 + at["y"]) * 4 + at["x"]


def shift(value, axis, step):
    if axis in ("z", "core"):
        name, size = "body", 8
        move = (lambda i: (i + 2 * step) % 8) if axis == "z" else (lambda i: i ^ 1)
    else:
        name, size = "blk", 16
        if axis == "y":
            move = lambda i: (i + 4 * step) % 16
        else:
            move = lambda i: i // 4 * 4 + (i + step) % 4
    return lax.ppermute(value, name, [(i, move(i)) for i in range(size)])


def offsets(order):
    grid = np.meshgrid(*[np.arange(2 if n == "f" else 4) for n in order], indexing="ij")
    return {n: g.reshape(-1) for n, g in zip(order, grid)}


def tables(here, mine, pattern):
    me = place(here)
    wanted, senders, takers = [], [], []
    for one, two, three in ORDERS:
        o = offsets(("1", "2", "f", "3"))
        at = dict(me)
        at[one], at[two], at[three] = ((me[n] + o[k]) % 4 for n, k in ((one, "1"), (two, "2"), (three, "3")))
        at["core"] = me["core"] ^ o["f"]
        wanted.append(number(at))
    for stage in (2, 3):
        for one, two, three in ORDERS:
            o = offsets(("1", "2", "f", "3") if stage == 2 else ("2", "1", "f", "3"))
            sender, taker = dict(me), dict(me)
            sender[one] = (me[one] - o["1"]) % 4
            if stage == 3:
                sender[two] = (me[two] - o["2"]) % 4
            else:
                taker[two] = (me[two] + o["2"]) % 4
            taker["core"] = me["core"] ^ o["f"]
            taker[three] = (me[three] + o["3"]) % 4
            senders.append(number(sender) + jnp.zeros((SLOTS,), jnp.int32))
            takers.append(number(taker) + jnp.zeros((SLOTS,), jnp.int32))
    wanted = jnp.concatenate(wanted)
    senders, takers = jnp.concatenate(senders), jnp.concatenate(takers)
    ids = jnp.arange(SLOTS, dtype=jnp.int32)
    chosen = jnp.max(jnp.where(ids[:, None] == wanted[None, :], mine[:, None], -1), axis=0)
    picked = dot((senders[:, None] == ids[None, :]).astype(jnp.bfloat16), (pattern + 1).astype(jnp.bfloat16))
    picked = jnp.sum(jnp.where(takers[:, None] == ids[None, :], picked, 0.0), axis=1).astype(jnp.int32) - 1
    second, third = picked.reshape(2, STREAMS, SLOTS)
    return chosen, second, third


def overflows(pattern):
    real = (pattern >= 0).astype(jnp.bfloat16)
    at = place(np.arange(SLOTS))
    firsts, lefts, rights = [], [], []
    for one, two, three in ORDERS:
        firsts.append(np.arange(4)[None, :] == at[one][:, None])
        lefts.append(np.arange(32)[:, None] == ((at["core"] * 4 + at[two]) * 4 + at[three])[None, :])
        rights.append(np.arange(16)[None, :] == (at[one] * 4 + at[two])[:, None])
    firsts = jnp.asarray(np.concatenate(firsts, 1), jnp.bfloat16)
    lefts = jnp.asarray(np.concatenate(lefts, 0), jnp.bfloat16)
    rights = jnp.asarray(np.concatenate(rights, 1), jnp.bfloat16)
    same = (np.arange(STREAMS * 32) // 32)[:, None] == (np.arange(STREAMS * 16) // 16)[None, :]
    one = jnp.max(dot(real, firsts))
    two = jnp.max(jnp.where(same, dot(dot(lefts, real).astype(jnp.bfloat16), rights), 0.0))
    return (one > FIRST) | (two > SECOND)


def shards(state, diag, nbr, near, donor, donor_src, donor_slot, donor_recv, phase):
    here = lax.axis_index("body") * lax.axis_size("blk") + lax.axis_index("blk")
    rows = lax.broadcasted_iota(jnp.int32, (SLOTS, donor.shape[0]), 0)
    hit = rows == donor_slot[None, :]
    mine = jnp.max(jnp.where(hit, lax.broadcasted_iota(jnp.int32, hit.shape, 1), -1), axis=1)
    recv = jnp.max(jnp.where(hit, donor_recv[None, :], -1), axis=1)
    spread = jnp.broadcast_to(recv[None, None, :], (SLOTS, 1, SLOTS))
    pattern = lax.all_to_all(spread, AXES, split_axis=0, concat_axis=0, tiled=True)[:, 0]
    chosen, second, third = tables(here, mine, pattern)
    near = near.reshape(-1)
    columns = lax.broadcasted_iota(jnp.int32, donor_src.shape, 1)
    sources = [jnp.sum(jnp.where(columns == phase[i], donor_src, 0), axis=1) for i in range(2)]
    state, chosen = lax.optimization_barrier((state, chosen, pattern))[:2]

    def dense(vectors, source):
        target = lax.dynamic_slice_in_dim(pattern, here, 1, axis=1)[:, 0]
        outgoing, inner = products(source, donor_slot, near, vectors, diag, nbr, donor, SLOTS)
        incoming = lax.all_to_all(outgoing, AXES, split_axis=0, concat_axis=0, tiled=True)
        return summed(target, inner, incoming)

    def staged(vectors, source):
        sent = donate(source, chosen, vectors, donor)
        inner = interior(near, vectors, diag, nbr)
        parts = []
        tied, inner = lax.optimization_barrier((second, inner))
        flight = [
            [sent[s * RING]] + [shift(sent[s * RING + k], ORDERS[s][0], k) for k in range(1, RING)]
            for s in range(STREAMS)
        ]
        passed = [relay(tied[s], flight[s]) for s in range(STREAMS)]
        flight = [
            [passed[s][0]] + [shift(passed[s][k], ORDERS[s][1], k) for k in range(1, RING)]
            for s in range(STREAMS)
        ]
        for s in range(STREAMS):
            own, flip = gathered(third[s], flight[s], vectors.shape[0])
            ready = joined(own, shift(flip, "core", 1))
            parts += [ready[0]] + [shift(ready[k], ORDERS[s][2], k) for k in range(1, RING)]
        return final(inner, parts)

    def all_dense():
        first = dense(state, sources[0])
        return first, dense(first, sources[1])

    first = staged(state, sources[0])
    second_out = staged(first, sources[1])
    return lax.cond(overflows(pattern), all_dense, lambda: (first, second_out))


def solution(mesh):
    split = P(AXES)
    return jax.shard_map(
        shards,
        mesh=mesh,
        in_specs=(split,) * 8 + (P(),),
        out_specs=(split, split),
        check_vma=False,
    )
```

```python
import functools

import jax
import jax.numpy as jnp
from jax import lax
from jax.experimental import pallas as pl
from jax.experimental.pallas import tpu as pltpu
from jax.sharding import PartitionSpec as P
import numpy as np

AXES = ("body", "blk")
ANY = pl.BlockSpec(memory_space=pl.ANY)
VMEM = pl.BlockSpec(memory_space=pltpu.VMEM)
SMEM = pl.BlockSpec(memory_space=pltpu.SMEM)
LIMIT = 40 * 1024 * 1024


def near_core(shape, kind):
    return pltpu.VMEM(shape, kind)


def pinned(values):
    return [pltpu.with_memory_space_constraint(v, pltpu.VMEM) for v in values]


GROUP = 4
SLOTS = 128
STREAMS, RING = 3, 4
REACH, CELL = 32, 8
FIRST, SECOND = 23, 25
ROWS = ((0, 112), (112, 112), (224, 96))
ORDERS = (("z", "y", "x"), ("y", "x", "z"), ("x", "z", "y"))


def dot(a, b):
    return jnp.dot(a, b, preferred_element_type=jnp.float32)


def product_kernel(source, slot, near, vectors, diag, nbr, donor, out, inner,
                   donor_buf, diag_buf, nbr_buf, made, donor_sem, diag_sem, nbr_sem, out_sem):
    count = donor.shape[0]
    blocks, fan = nbr.shape[0], nbr.shape[1]

    def donor_copy(g):
        part = pl.ds(g * GROUP, GROUP)
        return pltpu.make_async_copy(donor.at[part], donor_buf.at[part], donor_sem.at[g])

    def nbr_copy(b):
        return pltpu.make_async_copy(nbr.at[b], nbr_buf.at[b], nbr_sem.at[b])

    def out_copy(e):
        return pltpu.make_async_copy(made.at[e], out.at[slot[e]], out_sem.at[e])

    diag_copy = pltpu.make_async_copy(diag, diag_buf, diag_sem)
    for g in range(count // GROUP):
        donor_copy(g).start()
    diag_copy.start()
    for b in range(blocks):
        nbr_copy(b).start()

    @pl.loop(0, count // GROUP)
    def _(g):
        donor_copy(g).wait()
        for i in range(GROUP):
            e = g * GROUP + i
            made[e] = dot(donor_buf[e], vectors[source[e]]).astype(made.dtype)
            out_copy(e).start()

    diag_copy.wait()

    @pl.loop(0, blocks)
    def _(b):
        nbr_copy(b).wait()
        total = dot(diag_buf[b], vectors[b])
        for k in range(fan):
            total = total + dot(nbr_buf[b, k], vectors[near[b * fan + k]])
        inner[b] = total

    @pl.loop(0, count)
    def _(e):
        out_copy(e).wait()


def products(source, slot, near, vectors, diag, nbr, donor, slots):
    count = donor.shape[0]
    blocks, width, columns = vectors.shape
    return pl.pallas_call(
        product_kernel,
        out_shape=(
            jax.ShapeDtypeStruct((slots, width, columns), vectors.dtype),
            jax.ShapeDtypeStruct((blocks, width, columns), jnp.float32),
        ),
        in_specs=[SMEM, SMEM, SMEM, VMEM, ANY, ANY, ANY],
        out_specs=(ANY, VMEM),
        scratch_shapes=[
            pltpu.VMEM(donor.shape, donor.dtype),
            pltpu.VMEM(diag.shape, diag.dtype),
            pltpu.VMEM(nbr.shape, nbr.dtype),
            pltpu.VMEM((count, width, columns), vectors.dtype),
            pltpu.SemaphoreType.DMA((count // GROUP,)),
            pltpu.SemaphoreType.DMA,
            pltpu.SemaphoreType.DMA((blocks,)),
            pltpu.SemaphoreType.DMA((count,)),
        ],
        compiler_params=pltpu.CompilerParams(vmem_limit_bytes=LIMIT),
        name="products",
    )(source, slot, near, vectors, diag, nbr, donor)


def sum_kernel(target, inner, incoming, out, buf, total, sem):
    slots = incoming.shape[0]

    def copy(s):
        return pltpu.make_async_copy(incoming.at[s], buf.at[s], sem.at[s])

    @pl.loop(0, slots)
    def _(s):
        @pl.when(target[s] >= 0)
        def _():
            copy(s).start()

    total[...] = inner[...]

    @pl.loop(0, slots)
    def _(s):
        @pl.when(target[s] >= 0)
        def _():
            copy(s).wait()
            r = target[s]
            total[r] = total[r] + buf[s].astype(jnp.float32)

    out[...] = total[...].astype(out.dtype)


def summed(target, inner, incoming):
    return pl.pallas_call(
        sum_kernel,
        out_shape=jax.ShapeDtypeStruct(inner.shape, incoming.dtype),
        in_specs=[SMEM, VMEM, ANY],
        out_specs=VMEM,
        scratch_shapes=[
            pltpu.VMEM(incoming.shape, incoming.dtype),
            pltpu.VMEM(inner.shape, jnp.float32),
            pltpu.SemaphoreType.DMA((incoming.shape[0],)),
        ],
        compiler_params=pltpu.CompilerParams(vmem_limit_bytes=LIMIT),
        name="summed",
    )(target, inner, incoming)

def inner_kernel(near, vectors, diag, nbr, inner, diag_buf, nbr_buf, diag_sem, nbr_sem):
    blocks, fan = nbr.shape[0], nbr.shape[1]

    def nbr_copy(b):
        return pltpu.make_async_copy(nbr.at[b], nbr_buf.at[b], nbr_sem.at[b])

    diag_copy = pltpu.make_async_copy(diag, diag_buf, diag_sem)
    diag_copy.start()
    for b in range(blocks):
        nbr_copy(b).start()
    diag_copy.wait()

    @pl.loop(0, blocks)
    def _(b):
        nbr_copy(b).wait()
        total = dot(diag_buf[b], vectors[b])
        for k in range(fan):
            total = total + dot(nbr_buf[b, k], vectors[near[b * fan + k]])
        inner[b] = total


def interior(near, vectors, diag, nbr):
    blocks, width, columns = vectors.shape
    return pl.pallas_call(
        inner_kernel,
        out_shape=near_core((blocks, width, columns), jnp.float32),
        in_specs=[SMEM, VMEM, ANY, ANY],
        out_specs=VMEM,
        scratch_shapes=[
            pltpu.VMEM(diag.shape, diag.dtype),
            pltpu.VMEM(nbr.shape, nbr.dtype),
            pltpu.SemaphoreType.DMA,
            pltpu.SemaphoreType.DMA((blocks,)),
        ],
        compiler_params=pltpu.CompilerParams(vmem_limit_bytes=18 * 2**20),
        cost_estimate=pl.CostEstimate(flops=4 * 10**9, bytes_accessed=2 * 10**7, transcendentals=0),
        name="interior",
    )(near, vectors, diag, nbr)


def donate_kernel(source, chosen, vectors, donor, *refs):
    outs, refs = refs[:STREAMS * RING], refs[STREAMS * RING:]
    donor_buf, made, donor_sem = refs
    count = donor.shape[0]

    def donor_copy(g):
        part = pl.ds(g * GROUP, GROUP)
        return pltpu.make_async_copy(donor.at[part], donor_buf.at[part], donor_sem.at[g])

    for g in range(count // GROUP):
        donor_copy(g).start()

    @pl.loop(0, count // GROUP)
    def _(g):
        donor_copy(g).wait()
        for i in range(GROUP):
            e = g * GROUP + i
            made[e] = dot(donor_buf[e], vectors[source[e]]).astype(made.dtype)

    for s, (start, rows) in enumerate(ROWS):
        for k in range(RING):
            out = outs[s * RING + k]
            base = (s * RING + k) * REACH

            def step(j, held, out=out, base=base, start=start, rows=rows):
                e = chosen[base + j]

                @pl.when((e >= 0) & (held < FIRST))
                def _():
                    out[held] = made[e, pl.ds(start, rows)]

                return held + (e >= 0).astype(jnp.int32)

            lax.fori_loop(0, REACH, step, jnp.int32(0), unroll=4)


def donate(source, chosen, vectors, donor):
    count = donor.shape[0]
    width, columns = vectors.shape[1:]
    shapes = [(rows, columns) for _, rows in ROWS for _ in range(RING)]
    return pl.pallas_call(
        donate_kernel,
        out_shape=tuple(near_core((FIRST,) + s, vectors.dtype) for s in shapes),
        in_specs=[SMEM, SMEM, VMEM, ANY],
        out_specs=(VMEM,) * len(shapes),
        scratch_shapes=[
            pltpu.VMEM(donor.shape, donor.dtype),
            pltpu.VMEM((count, width, columns), vectors.dtype),
            pltpu.SemaphoreType.DMA((count // GROUP,)),
        ],
        compiler_params=pltpu.CompilerParams(vmem_limit_bytes=28 * 2**20),
        name="donate",
    )(source, chosen, vectors, donor)


def relay_kernel(row, table, *refs):
    ins, outs = refs[:RING], refs[RING:]
    held = [jnp.int32(0)] * RING
    for i in range(RING):
        taken = jnp.int32(0)
        for k in range(RING):

            def step(j, both, i=i, k=k):
                into, out_of = both
                real = table[row, (i * RING + k) * CELL + j] >= 0

                @pl.when(real & (into < SECOND) & (out_of < FIRST))
                def _():
                    outs[k][into] = ins[i][out_of]

                one = real.astype(jnp.int32)
                return into + one, out_of + one

            held[k], taken = lax.fori_loop(0, CELL, step, (held[k], taken), unroll=1)


def relay(table, row, ins):
    shape, kind = ins[0].shape[1:], ins[0].dtype
    return pl.pallas_call(
        functools.partial(relay_kernel, row),
        out_shape=(near_core((SECOND,) + shape, kind),) * RING,
        in_specs=[SMEM] + [VMEM] * RING,
        out_specs=(VMEM,) * RING,
        compiler_params=pltpu.CompilerParams(vmem_limit_bytes=8 * 2**20),
        cost_estimate=pl.CostEstimate(flops=10**6, bytes_accessed=6 * 10**6, transcendentals=0),
        name="relay",
    )(table, *pinned(ins))


def gather_kernel(row, table, *refs):
    ins, (own, flip, total) = refs[:RING], refs[RING:]
    blocks = own.shape[0] // RING

    @pl.loop(0, RING * blocks)
    def _(cell):
        own[cell] = jnp.zeros(own.shape[1:], own.dtype)
        total[cell] = jnp.zeros(own.shape[1:], own.dtype)

    for i in range(RING):

        def step(q, taken, i=i):
            for f, sums in ((0, own), (1, total)):
                for k in range(RING):
                    r = table[row, ((i * RING + q) * 2 + f) * RING + k]
                    real = r >= 0

                    @pl.when(real & (taken < SECOND))
                    def _(taken=taken, cell=k * blocks + r, sums=sums):
                        sums[cell] = sums[cell] + ins[i][taken].astype(jnp.float32)

                    taken = taken + real.astype(jnp.int32)
            return taken

        lax.fori_loop(0, RING, step, jnp.int32(0))

    @pl.loop(0, RING * blocks, unroll=2)
    def _(cell):
        flip[cell] = total[cell].astype(flip.dtype)


def gathered(table, row, ins, blocks):
    shape, kind = ins[0].shape[1:], ins[0].dtype
    return pl.pallas_call(
        functools.partial(gather_kernel, row),
        out_shape=(
            near_core((RING * blocks,) + shape, jnp.float32),
            near_core((RING * blocks,) + shape, kind),
        ),
        in_specs=[SMEM] + [VMEM] * RING,
        out_specs=(VMEM, VMEM),
        scratch_shapes=[pltpu.VMEM((RING * blocks,) + shape, jnp.float32)],
        compiler_params=pltpu.CompilerParams(vmem_limit_bytes=12 * 2**20),
        cost_estimate=pl.CostEstimate(flops=10**6, bytes_accessed=6 * 10**6, transcendentals=0),
        name="gathered",
    )(table, *pinned(ins))


def join_kernel(own, flip, *outs):
    blocks = outs[0].shape[0]

    @pl.loop(0, blocks)
    def _(b):
        for k in range(RING):
            both = own[k * blocks + b] + flip[k * blocks + b].astype(jnp.float32)
            outs[k][b] = both.astype(outs[k].dtype)


def joined(own, flip):
    blocks = own.shape[0] // RING
    return pl.pallas_call(
        join_kernel,
        out_shape=(near_core((blocks,) + own.shape[1:], flip.dtype),) * RING,
        in_specs=[VMEM, VMEM],
        out_specs=(VMEM,) * RING,
        compiler_params=pltpu.CompilerParams(vmem_limit_bytes=8 * 2**20),
        cost_estimate=pl.CostEstimate(flops=10**6, bytes_accessed=5 * 10**6, transcendentals=0),
        name="joined",
    )(*pinned((own, flip)))


def final_kernel(inner, *refs):
    parts, out = refs[:-1], refs[-1]

    @pl.loop(0, out.shape[0])
    def _(b):
        for s, (start, rows) in enumerate(ROWS):
            part = pl.ds(start, rows)
            total = inner[b, part]
            for k in range(RING):
                total = total + parts[s * RING + k][b].astype(jnp.float32)
            out[b, part] = total.astype(out.dtype)


def final(inner, parts):
    return pl.pallas_call(
        final_kernel,
        out_shape=jax.ShapeDtypeStruct(inner.shape, parts[0].dtype),
        in_specs=[VMEM] * (1 + len(parts)),
        out_specs=VMEM,
        compiler_params=pltpu.CompilerParams(vmem_limit_bytes=12 * 2**20),
        name="final",
    )(*pinned((inner, *parts)))


def place(index):
    return {"z": index // 32, "core": index // 16 % 2, "y": index // 4 % 4, "x": index % 4}


def number(at):
    return ((at["z"] * 2 + at["core"]) * 4 + at["y"]) * 4 + at["x"]


def shift(value, axis, step):
    if axis in ("z", "core"):
        name, size = "body", 8
        move = (lambda i: (i + 2 * step) % 8) if axis == "z" else (lambda i: i ^ 1)
    else:
        name, size = "blk", 16
        if axis == "y":
            move = lambda i: (i + 4 * step) % 16
        else:
            move = lambda i: i // 4 * 4 + (i + step) % 4
    return lax.ppermute(value, name, [(i, move(i)) for i in range(size)])


def offsets(order):
    grid = np.meshgrid(*[np.arange(2 if n == "f" else 4) for n in order], indexing="ij")
    return {n: g.reshape(-1) for n, g in zip(order, grid)}


def spots(stage):
    senders, takers = [], []
    for one, two, three in ORDERS:
        o = offsets(("2", "1", "f", "3") if stage == 3 else ("1", "2", "f", "3"))
        sender = {n: np.zeros(SLOTS, np.int64) for n in ("z", "core", "y", "x")}
        taker = {n: np.zeros(SLOTS, np.int64) for n in ("z", "core", "y", "x")}
        if stage == 1:
            taker[one] = o["1"]
        else:
            sender[one] = -o["1"] % 4
        if stage == 3:
            sender[two] = -o["2"] % 4
        else:
            taker[two] = o["2"]
        taker["core"], taker[three] = o["f"], o["3"]
        senders.append(number(sender))
        takers.append(number(taker))
    return np.concatenate(senders).astype(np.int32), np.concatenate(takers).astype(np.int32)


def moved(here, step):
    me, step = place(here), place(step)
    return number({n: (me[n] ^ step[n]) if n == "core" else (me[n] + step[n]) % 4 for n in me})


def choices(here, mine):
    ids = jnp.arange(SLOTS, dtype=jnp.int32)
    wanted = moved(here, jnp.asarray(spots(1)[1]))
    return jnp.max(jnp.where(ids[:, None] == wanted[None, :], mine[:, None], -1), axis=0)


def table_kernel(here, pattern, senders, takers, firsts, lefts, rights, same, out):
    def spread(index):
        return index >> 5, (index >> 4) & 1, (index >> 2) & 3, index & 3

    def move(step):
        mine, step = spread(here[0]), spread(step)
        z, y, x = ((mine[i] + step[i]) & 3 for i in (0, 2, 3))
        return ((z * 2 + (mine[1] ^ step[1])) * 4 + y) * 4 + x

    whole = pattern[...].astype(jnp.float32)
    ids = lax.broadcasted_iota(jnp.int32, (SLOTS, senders.shape[1]), 0)
    one_hot = jnp.where(ids == move(senders[...]), 1.0, 0.0).astype(jnp.bfloat16)
    picked = lax.dot_general(
        (whole + 1.0).astype(jnp.bfloat16), one_hot, (((0,), (0,)), ((), ())),
        preferred_element_type=jnp.float32,
    )
    picked = jnp.sum(jnp.where(ids == move(takers[...]), picked, 0.0), axis=0, keepdims=True) - 1.0
    for row in range(2 * STREAMS):
        out[pl.ds(row, 1)] = picked[:, row * SLOTS:(row + 1) * SLOTS].astype(jnp.int32)
    real = jnp.where(whole >= 0.0, 1.0, 0.0).astype(jnp.bfloat16)
    one = jnp.max(dot(real, firsts[...]), keepdims=True) - FIRST
    two = dot(dot(lefts[...], real).astype(jnp.bfloat16), rights[...]) * same[...]
    over = jnp.maximum(one, jnp.max(two, keepdims=True) - SECOND)
    out[pl.ds(2 * STREAMS, 1)] = jnp.broadcast_to(over, (1, SLOTS)).astype(jnp.int32)


def tables(here, pattern):
    senders, takers = (np.concatenate(pair)[None, :] for pair in zip(spots(2), spots(3)))
    at = place(np.arange(SLOTS))
    firsts, lefts, rights = [], [], []
    for one, two, three in ORDERS:
        firsts.append(np.arange(4)[None, :] == at[one][:, None])
        lefts.append(np.arange(32)[:, None] == ((at["core"] * 4 + at[two]) * 4 + at[three])[None, :])
        rights.append(np.arange(16)[None, :] == (at[one] * 4 + at[two])[:, None])
    same = (np.arange(STREAMS * 32) // 32)[:, None] == (np.arange(STREAMS * 16) // 16)[None, :]
    return pl.pallas_call(
        table_kernel,
        out_shape=jax.ShapeDtypeStruct((8, SLOTS), jnp.int32),
        in_specs=[SMEM] + [VMEM] * 7,
        out_specs=VMEM,
        compiler_params=pltpu.CompilerParams(vmem_limit_bytes=8 * 2**20),
        name="tables",
    )(
        here.reshape(1),
        pattern,
        jnp.asarray(senders),
        jnp.asarray(takers),
        jnp.asarray(np.concatenate(firsts, 1), jnp.bfloat16),
        jnp.asarray(np.concatenate(lefts, 0), jnp.bfloat16),
        jnp.asarray(np.concatenate(rights, 1), jnp.bfloat16),
        jnp.asarray(same, jnp.float32),
    )


def shards(state, diag, nbr, near, donor, donor_src, donor_slot, donor_recv, phase):
    here = lax.axis_index("body") * lax.axis_size("blk") + lax.axis_index("blk")
    rows = lax.broadcasted_iota(jnp.int32, (SLOTS, donor.shape[0]), 0)
    hit = rows == donor_slot[None, :]
    mine = jnp.max(jnp.where(hit, lax.broadcasted_iota(jnp.int32, hit.shape, 1), -1), axis=1)
    recv = jnp.max(jnp.where(hit, donor_recv[None, :], -1), axis=1)
    spread = jnp.broadcast_to(recv[None, None, :], (SLOTS, 1, SLOTS))
    pattern = lax.all_to_all(spread, AXES, split_axis=0, concat_axis=0, tiled=True)[:, 0]
    chosen = choices(here, mine)
    near = near.reshape(-1)
    columns = lax.broadcasted_iota(jnp.int32, donor_src.shape, 1)
    sources = [jnp.sum(jnp.where(columns == phase[i], donor_src, 0), axis=1) for i in range(2)]
    held = (state, chosen, pattern, near, here, *sources)
    state, chosen, pattern, near, here, *sources = lax.optimization_barrier(held)

    def dense(vectors, source):
        target = lax.dynamic_slice_in_dim(pattern, here, 1, axis=1)[:, 0]
        outgoing, inner = products(source, donor_slot, near, vectors, diag, nbr, donor, SLOTS)
        incoming = lax.all_to_all(outgoing, AXES, split_axis=0, concat_axis=0, tiled=True)
        out = summed(target, inner, incoming)
        return out, out

    def all_dense():
        return tuple(lax.scan(dense, state, jnp.stack(sources))[1])

    def staged(vectors, source, plan):
        sent = donate(source, chosen, vectors, donor)
        if plan is None:
            plan = tables(here, pattern)
        inner = interior(near, vectors, diag, nbr)
        parts = []
        inner, plan = lax.optimization_barrier((inner, plan))
        flight = [
            [sent[s * RING]] + [shift(sent[s * RING + k], ORDERS[s][0], k) for k in range(1, RING)]
            for s in range(STREAMS)
        ]
        passed = [relay(plan, s, flight[s]) for s in range(STREAMS)]
        flight = [
            [passed[s][0]] + [shift(passed[s][k], ORDERS[s][1], k) for k in range(1, RING)]
            for s in range(STREAMS)
        ]
        for s in range(STREAMS):
            own, flip = gathered(plan, STREAMS + s, flight[s], vectors.shape[0])
            ready = joined(own, shift(flip, "core", 1))
            parts += [ready[0]] + [shift(ready[k], ORDERS[s][2], k) for k in range(1, RING)]
        return final(inner, parts), plan

    first, plan = staged(state, sources[0], None)
    second, _ = staged(first, sources[1], plan)
    return lax.cond(plan[2 * STREAMS, 0] > 0, all_dense, lambda: (first, second))


def solution(mesh):
    split = P(AXES)
    return jax.shard_map(
        shards,
        mesh=mesh,
        in_specs=(split,) * 8 + (P(),),
        out_specs=(split, split),
        check_vma=False,
    )
```

```python
import functools

import jax
import jax.numpy as jnp
from jax import lax
from jax.experimental import pallas as pl
from jax.experimental.pallas import tpu as pltpu
from jax.sharding import PartitionSpec as P
import numpy as np

AXES = ("body", "blk")
ANY = pl.BlockSpec(memory_space=pl.ANY)
VMEM = pl.BlockSpec(memory_space=pltpu.VMEM)
SMEM = pl.BlockSpec(memory_space=pltpu.SMEM)
LIMIT = 40 * 1024 * 1024


def near_core(shape, kind):
    return pltpu.VMEM(shape, kind)


def pinned(values):
    return [pltpu.with_memory_space_constraint(v, pltpu.VMEM) for v in values]


GROUP = 4
SLOTS = 128
STREAMS, RING = 3, 4
REACH, CELL, NEAR, PHASES = 32, 8, 12, 4
FIRST, SECOND = 23, 25
ROWS = ((0, 112), (112, 112), (224, 96))
ORDERS = (("z", "y", "x"), ("y", "x", "z"), ("x", "z", "y"))


def dot(a, b):
    return jnp.dot(a, b, preferred_element_type=jnp.float32)


def product_kernel(source, slot, near, vectors, diag, nbr, donor, out, inner,
                   donor_buf, diag_buf, nbr_buf, made, donor_sem, diag_sem, nbr_sem, out_sem):
    count = donor.shape[0]
    blocks, fan = nbr.shape[0], nbr.shape[1]

    def donor_copy(g):
        part = pl.ds(g * GROUP, GROUP)
        return pltpu.make_async_copy(donor.at[part], donor_buf.at[part], donor_sem.at[g])

    def nbr_copy(b):
        return pltpu.make_async_copy(nbr.at[b], nbr_buf.at[b], nbr_sem.at[b])

    def out_copy(e):
        return pltpu.make_async_copy(made.at[e], out.at[slot[e]], out_sem.at[e])

    diag_copy = pltpu.make_async_copy(diag, diag_buf, diag_sem)
    for g in range(count // GROUP):
        donor_copy(g).start()
    diag_copy.start()
    for b in range(blocks):
        nbr_copy(b).start()

    @pl.loop(0, count // GROUP)
    def _(g):
        donor_copy(g).wait()
        for i in range(GROUP):
            e = g * GROUP + i
            made[e] = dot(donor_buf[e], vectors[source[e]]).astype(made.dtype)
            out_copy(e).start()

    diag_copy.wait()

    @pl.loop(0, blocks)
    def _(b):
        nbr_copy(b).wait()
        total = dot(diag_buf[b], vectors[b])
        for k in range(fan):
            total = total + dot(nbr_buf[b, k], vectors[near[b * fan + k]])
        inner[b] = total

    @pl.loop(0, count)
    def _(e):
        out_copy(e).wait()


def products(source, slot, near, vectors, diag, nbr, donor, slots):
    count = donor.shape[0]
    blocks, width, columns = vectors.shape
    return pl.pallas_call(
        product_kernel,
        out_shape=(
            jax.ShapeDtypeStruct((slots, width, columns), vectors.dtype),
            jax.ShapeDtypeStruct((blocks, width, columns), jnp.float32),
        ),
        in_specs=[SMEM, SMEM, SMEM, VMEM, ANY, ANY, ANY],
        out_specs=(ANY, VMEM),
        scratch_shapes=[
            pltpu.VMEM(donor.shape, donor.dtype),
            pltpu.VMEM(diag.shape, diag.dtype),
            pltpu.VMEM(nbr.shape, nbr.dtype),
            pltpu.VMEM((count, width, columns), vectors.dtype),
            pltpu.SemaphoreType.DMA((count // GROUP,)),
            pltpu.SemaphoreType.DMA,
            pltpu.SemaphoreType.DMA((blocks,)),
            pltpu.SemaphoreType.DMA((count,)),
        ],
        compiler_params=pltpu.CompilerParams(vmem_limit_bytes=LIMIT),
        name="products",
    )(source, slot, near, vectors, diag, nbr, donor)


def sum_kernel(target, inner, incoming, out, buf, total, sem):
    slots = incoming.shape[0]

    def copy(s):
        return pltpu.make_async_copy(incoming.at[s], buf.at[s], sem.at[s])

    @pl.loop(0, slots)
    def _(s):
        @pl.when(target[s] >= 0)
        def _():
            copy(s).start()

    total[...] = inner[...]

    @pl.loop(0, slots)
    def _(s):
        @pl.when(target[s] >= 0)
        def _():
            copy(s).wait()
            r = target[s]
            total[r] = total[r] + buf[s].astype(jnp.float32)

    out[...] = total[...].astype(out.dtype)


def summed(target, inner, incoming):
    return pl.pallas_call(
        sum_kernel,
        out_shape=jax.ShapeDtypeStruct(inner.shape, incoming.dtype),
        in_specs=[SMEM, VMEM, ANY],
        out_specs=VMEM,
        scratch_shapes=[
            pltpu.VMEM(incoming.shape, incoming.dtype),
            pltpu.VMEM(inner.shape, jnp.float32),
            pltpu.SemaphoreType.DMA((incoming.shape[0],)),
        ],
        compiler_params=pltpu.CompilerParams(vmem_limit_bytes=LIMIT),
        name="summed",
    )(target, inner, incoming)

def inner_kernel(near, vectors, diag, nbr, inner, diag_buf, nbr_buf, diag_sem, nbr_sem):
    blocks, fan = nbr.shape[0], nbr.shape[1]

    def nbr_copy(b):
        return pltpu.make_async_copy(nbr.at[b], nbr_buf.at[b], nbr_sem.at[b])

    diag_copy = pltpu.make_async_copy(diag, diag_buf, diag_sem)
    diag_copy.start()
    for b in range(blocks):
        nbr_copy(b).start()
    diag_copy.wait()

    @pl.loop(0, blocks)
    def _(b):
        nbr_copy(b).wait()
        total = dot(diag_buf[b], vectors[b])
        for k in range(fan):
            total = total + dot(nbr_buf[b, k], vectors[near[b * fan + k]])
        inner[b] = total


def interior(near, vectors, diag, nbr):
    blocks, width, columns = vectors.shape
    return pl.pallas_call(
        inner_kernel,
        out_shape=near_core((blocks, width, columns), jnp.float32),
        in_specs=[SMEM, VMEM, ANY, ANY],
        out_specs=VMEM,
        scratch_shapes=[
            pltpu.VMEM(diag.shape, diag.dtype),
            pltpu.VMEM(nbr.shape, nbr.dtype),
            pltpu.SemaphoreType.DMA,
            pltpu.SemaphoreType.DMA((blocks,)),
        ],
        compiler_params=pltpu.CompilerParams(vmem_limit_bytes=18 * 2**20),
        cost_estimate=pl.CostEstimate(flops=4 * 10**9, bytes_accessed=2 * 10**7, transcendentals=0),
        name="interior",
    )(near, vectors, diag, nbr)


def donate_kernel(turn, phase, source, table, vectors, donor, *refs):
    outs, refs = refs[:STREAMS * RING], refs[STREAMS * RING:]
    donor_buf, made, donor_sem = refs
    count = donor.shape[0]

    def donor_copy(g):
        part = pl.ds(g * GROUP, GROUP)
        return pltpu.make_async_copy(donor.at[part], donor_buf.at[part], donor_sem.at[g])

    for g in range(count // GROUP):
        donor_copy(g).start()

    @pl.loop(0, count // GROUP)
    def _(g):
        donor_copy(g).wait()
        for i in range(GROUP):
            e = g * GROUP + i
            made[e] = dot(donor_buf[e], vectors[source[e * PHASES + phase[turn]]]).astype(made.dtype)

    for s, (start, rows) in enumerate(ROWS):
        for k in range(RING):
            out = outs[s * RING + k]
            @pl.loop(0, jnp.minimum(table[3 * STREAMS + s, k], FIRST))
            def _(j, out=out, s=s, k=k, start=start, rows=rows):
                out[j] = made[table[s, k * REACH + j], pl.ds(start, rows)]


def donate(turn, phase, source, table, vectors, donor):
    count = donor.shape[0]
    width, columns = vectors.shape[1:]
    shapes = [(rows, columns) for _, rows in ROWS for _ in range(RING)]
    return pl.pallas_call(
        functools.partial(donate_kernel, turn),
        out_shape=tuple(near_core((FIRST,) + s, vectors.dtype) for s in shapes),
        in_specs=[SMEM, SMEM, SMEM, VMEM, ANY],
        out_specs=(VMEM,) * len(shapes),
        scratch_shapes=[
            pltpu.VMEM(donor.shape, donor.dtype),
            pltpu.VMEM((count, width, columns), vectors.dtype),
            pltpu.SemaphoreType.DMA((count // GROUP,)),
        ],
        compiler_params=pltpu.CompilerParams(vmem_limit_bytes=28 * 2**20),
        name="donate",
    )(phase, source, table, vectors, donor)


def relay_kernel(row, table, *refs):
    ins, outs = refs[:RING], refs[RING:]
    held = [jnp.int32(0)] * RING
    for i in range(RING):
        taken = jnp.int32(0)
        for k in range(RING):
            count = table[2 * STREAMS + row, i * RING + k]

            @pl.loop(0, jnp.minimum(count, jnp.minimum(FIRST - taken, SECOND - held[k])))
            def _(j, i=i, k=k, into=held[k], out_of=taken):
                outs[k][into + j] = ins[i][out_of + j]

            held[k], taken = held[k] + count, taken + count


def relay(table, row, ins):
    shape, kind = ins[0].shape[1:], ins[0].dtype
    return pl.pallas_call(
        functools.partial(relay_kernel, row),
        out_shape=(near_core((SECOND,) + shape, kind),) * RING,
        in_specs=[SMEM] + [VMEM] * RING,
        out_specs=(VMEM,) * RING,
        compiler_params=pltpu.CompilerParams(vmem_limit_bytes=8 * 2**20),
        cost_estimate=pl.CostEstimate(flops=10**6, bytes_accessed=6 * 10**6, transcendentals=0),
        name="relay",
    )(table, *pinned(ins))


def gather_kernel(row, table, *refs):
    ins, (own, flip, total) = refs[:RING], refs[RING:]
    blocks = own.shape[0] // RING

    @pl.loop(0, 2 * RING * blocks, unroll=2)
    def _(cell):
        total[cell] = jnp.zeros(total.shape[1:], total.dtype)

    for i in range(RING):

        @pl.loop(0, jnp.minimum(table[4 * STREAMS + row, i], SECOND))
        def _(j, i=i):
            cell = table[STREAMS + row, i * REACH + j]
            total[cell] = total[cell] + ins[i][j].astype(jnp.float32)

    @pl.loop(0, RING * blocks, unroll=2)
    def _(cell):
        own[cell] = total[cell].astype(own.dtype)
        flip[cell] = total[RING * blocks + cell].astype(flip.dtype)


def gathered(table, row, ins, blocks):
    shape, kind = ins[0].shape[1:], ins[0].dtype
    return pl.pallas_call(
        functools.partial(gather_kernel, row),
        out_shape=(
            near_core((RING * blocks,) + shape, kind),
            near_core((RING * blocks,) + shape, kind),
        ),
        in_specs=[SMEM] + [VMEM] * RING,
        out_specs=(VMEM, VMEM),
        scratch_shapes=[pltpu.VMEM((2 * RING * blocks,) + shape, jnp.float32)],
        compiler_params=pltpu.CompilerParams(vmem_limit_bytes=12 * 2**20),
        cost_estimate=pl.CostEstimate(flops=10**6, bytes_accessed=6 * 10**6, transcendentals=0),
        name="gathered",
    )(table, *pinned(ins))


def join_kernel(own, flip, *outs):
    blocks = outs[0].shape[0]

    @pl.loop(0, blocks)
    def _(b):
        for k in range(RING):
            both = own[k * blocks + b].astype(jnp.float32) + flip[k * blocks + b].astype(jnp.float32)
            outs[k][b] = both.astype(outs[k].dtype)


def joined(own, flip):
    blocks = own.shape[0] // RING
    return pl.pallas_call(
        join_kernel,
        out_shape=(near_core((blocks,) + own.shape[1:], flip.dtype),) * RING,
        in_specs=[VMEM, VMEM],
        out_specs=(VMEM,) * RING,
        compiler_params=pltpu.CompilerParams(vmem_limit_bytes=8 * 2**20),
        cost_estimate=pl.CostEstimate(flops=10**6, bytes_accessed=5 * 10**6, transcendentals=0),
        name="joined",
    )(*pinned((own, flip)))


def final_kernel(inner, *refs):
    parts, out = refs[:-1], refs[-1]

    @pl.loop(0, out.shape[0])
    def _(b):
        for s, (start, rows) in enumerate(ROWS):
            part = pl.ds(start, rows)
            total = inner[b, part]
            for k in range(RING):
                total = total + parts[s * RING + k][b].astype(jnp.float32)
            out[b, part] = total.astype(out.dtype)


def final(inner, parts):
    return pl.pallas_call(
        final_kernel,
        out_shape=jax.ShapeDtypeStruct(inner.shape, parts[0].dtype),
        in_specs=[VMEM] * (1 + len(parts)),
        out_specs=VMEM,
        compiler_params=pltpu.CompilerParams(vmem_limit_bytes=12 * 2**20),
        name="final",
    )(*pinned((inner, *parts)))


def place(index):
    return {"z": index // 32, "core": index // 16 % 2, "y": index // 4 % 4, "x": index % 4}


def number(at):
    return ((at["z"] * 2 + at["core"]) * 4 + at["y"]) * 4 + at["x"]


def shift(value, axis, step):
    if axis in ("z", "core"):
        name, size = "body", 8
        move = (lambda i: (i + 2 * step) % 8) if axis == "z" else (lambda i: i ^ 1)
    else:
        name, size = "blk", 16
        if axis == "y":
            move = lambda i: (i + 4 * step) % 16
        else:
            move = lambda i: i // 4 * 4 + (i + step) % 4
    return lax.ppermute(value, name, [(i, move(i)) for i in range(size)])


def offsets(order):
    grid = np.meshgrid(*[np.arange(2 if n == "f" else 4) for n in order], indexing="ij")
    return {n: g.reshape(-1) for n, g in zip(order, grid)}


def spots(stage):
    senders, takers = [], []
    for one, two, three in ORDERS:
        o = offsets(("2", "1", "f", "3") if stage == 3 else ("1", "2", "f", "3"))
        sender = {n: np.zeros(SLOTS, np.int64) for n in ("z", "core", "y", "x")}
        taker = {n: np.zeros(SLOTS, np.int64) for n in ("z", "core", "y", "x")}
        if stage == 1:
            taker[one] = o["1"]
        else:
            sender[one] = -o["1"] % 4
        if stage == 3:
            sender[two] = -o["2"] % 4
        else:
            taker[two] = o["2"]
        taker["core"], taker[three] = o["f"], o["3"]
        senders.append(number(sender))
        takers.append(number(taker))
    return np.concatenate(senders).astype(np.int32), np.concatenate(takers).astype(np.int32)


def moved(here, step):
    me, step = place(here), place(step)
    return number({n: (me[n] ^ step[n]) if n == "core" else (me[n] + step[n]) % 4 for n in me})


def table_kernel(here, slot, pattern, wanted, senders, takers, firsts, lefts, rights, same, out):
    def spread(index):
        return index >> 5, (index >> 4) & 1, (index >> 2) & 3, index & 3

    def move(step):
        mine, step = spread(here[0]), spread(step)
        z, y, x = ((mine[i] + step[i]) & 3 for i in (0, 2, 3))
        return ((z * 2 + (mine[1] ^ step[1])) * 4 + y) * 4 + x

    def ones(mask):
        return jnp.where(mask, 1.0, 0.0).astype(jnp.bfloat16)

    def rows(flat):
        return [flat[:, i * SLOTS:(i + 1) * SLOTS] for i in range(flat.shape[1] // SLOTS)]

    def put(row, value):
        out[pl.ds(row, 1)] = value.astype(jnp.int32)

    count = slot.shape[1]
    tile = lax.broadcasted_iota(jnp.int32, (SLOTS, count), 1).astype(jnp.float32) + 1.0
    hit = lax.broadcasted_iota(jnp.int32, (SLOTS, count), 0) == slot[...]
    tile = jnp.max(jnp.where(hit, tile, 0.0), axis=1, keepdims=True)
    ids = lax.broadcasted_iota(jnp.int32, (SLOTS, wanted.shape[1]), 0)
    chosen = jnp.sum(jnp.where(ids == move(wanted[...]), tile, 0.0), axis=0, keepdims=True) - 1.0

    whole = pattern[...].astype(jnp.float32)
    ids = lax.broadcasted_iota(jnp.int32, (SLOTS, senders.shape[1]), 0)
    picked = lax.dot_general(
        (whole + 1.0).astype(jnp.bfloat16), ones(ids == move(senders[...])), (((0,), (0,)), ((), ())),
        preferred_element_type=jnp.float32,
    )
    picked = jnp.sum(jnp.where(ids == move(takers[...]), picked, 0.0), axis=0, keepdims=True) - 1.0

    down = lax.broadcasted_iota(jnp.int32, (SLOTS, SLOTS), 0)
    across = lax.broadcasted_iota(jnp.int32, (SLOTS, SLOTS), 1)
    before = ones((down < across) & (down // REACH == across // REACH))
    lane = lax.broadcasted_iota(jnp.int32, (1, SLOTS), 1)
    cell = ((lane >> 2) & 1) * (RING * NEAR) + (lane & 3) * NEAR
    picked = rows(picked)
    for row, value in enumerate(rows(chosen) + picked[STREAMS:]):
        real = value >= 0.0
        if row >= STREAMS:
            value = value + cell.astype(jnp.float32)
        valid = jnp.broadcast_to(ones(real), (8, SLOTS))
        rank = dot(valid, before)[:1].astype(jnp.int32)
        spot = jnp.where(real, (lane & -REACH) + rank, -1)
        value = jnp.broadcast_to(value.astype(jnp.bfloat16), (8, SLOTS))
        put(row, lax.dot_general(
            value, ones(down == spot), (((1,), (1,)), ((), ())), preferred_element_type=jnp.float32
        )[:1])
        put(3 * STREAMS + row, dot(valid, ones(down // REACH == across))[:1])
    for row in range(STREAMS):
        valid = jnp.broadcast_to(ones(picked[row] >= 0.0), (8, SLOTS))
        put(2 * STREAMS + row, dot(valid, ones(down // CELL == across))[:1])

    real = ones(whole >= 0.0)
    one = jnp.max(dot(real, firsts[...]), keepdims=True) - FIRST
    two = dot(dot(lefts[...], real).astype(jnp.bfloat16), rights[...]) * same[...]
    over = jnp.maximum(one, jnp.max(two, keepdims=True) - SECOND)
    put(5 * STREAMS, jnp.broadcast_to(over, (1, SLOTS)))


def tables(here, slot, pattern):
    wanted = spots(1)[1][None, :]
    senders, takers = (np.concatenate(pair)[None, :] for pair in zip(spots(2), spots(3)))
    at = place(np.arange(SLOTS))
    firsts, lefts, rights = [], [], []
    for one, two, three in ORDERS:
        firsts.append(np.arange(4)[None, :] == at[one][:, None])
        lefts.append(np.arange(32)[:, None] == ((at["core"] * 4 + at[two]) * 4 + at[three])[None, :])
        rights.append(np.arange(16)[None, :] == (at[one] * 4 + at[two])[:, None])
    same = (np.arange(STREAMS * 32) // 32)[:, None] == (np.arange(STREAMS * 16) // 16)[None, :]
    return pl.pallas_call(
        table_kernel,
        out_shape=jax.ShapeDtypeStruct((16, SLOTS), jnp.int32),
        in_specs=[SMEM] + [VMEM] * 9,
        out_specs=VMEM,
        compiler_params=pltpu.CompilerParams(vmem_limit_bytes=12 * 2**20),
        name="tables",
    )(
        here.reshape(1),
        slot.reshape(1, -1),
        pattern,
        jnp.asarray(wanted),
        jnp.asarray(senders),
        jnp.asarray(takers),
        jnp.asarray(np.concatenate(firsts, 1), jnp.bfloat16),
        jnp.asarray(np.concatenate(lefts, 0), jnp.bfloat16),
        jnp.asarray(np.concatenate(rights, 1), jnp.bfloat16),
        jnp.asarray(same, jnp.float32),
    )


def shards(state, diag, nbr, near, donor, donor_src, donor_slot, donor_recv, phase):
    here = lax.axis_index("body") * lax.axis_size("blk") + lax.axis_index("blk")
    rows = lax.broadcasted_iota(jnp.int32, (SLOTS, donor.shape[0]), 0)
    hit = rows == donor_slot[None, :]
    recv = jnp.max(jnp.where(hit, donor_recv[None, :], -1), axis=1)
    spread = jnp.broadcast_to(recv[None, None, :], (SLOTS, 1, SLOTS))
    pattern = lax.all_to_all(spread, AXES, split_axis=0, concat_axis=0, tiled=True)[:, 0]
    flat = near.reshape(-1), donor_src.reshape(-1)
    near_flat, by_phase, state, pattern = lax.optimization_barrier((*flat, state, pattern))
    plan = tables(here, donor_slot, pattern)

    def dense(vectors, column):
        source = lax.dynamic_slice_in_dim(donor_src, column, 1, axis=1)[:, 0]
        target = lax.dynamic_slice_in_dim(pattern, here, 1, axis=1)[:, 0]
        outgoing, inner = products(source, donor_slot, near_flat, vectors, diag, nbr, donor, SLOTS)
        incoming = lax.all_to_all(outgoing, AXES, split_axis=0, concat_axis=0, tiled=True)
        out = summed(target, inner, incoming)
        return out, out

    def all_dense():
        return tuple(lax.scan(dense, state, phase)[1])

    def staged(turn, vectors):
        sent = donate(turn, phase, by_phase, plan, vectors, donor)
        inner = interior(near_flat, vectors, diag, nbr)
        parts = []
        inner, tied = lax.optimization_barrier((inner, plan))
        flight = [
            [sent[s * RING]] + [shift(sent[s * RING + k], ORDERS[s][0], k) for k in range(1, RING)]
            for s in range(STREAMS)
        ]
        passed = [relay(tied, s, flight[s]) for s in range(STREAMS)]
        flight = [
            [passed[s][0]] + [shift(passed[s][k], ORDERS[s][1], k) for k in range(1, RING)]
            for s in range(STREAMS)
        ]
        for s in range(STREAMS):
            own, flip = gathered(plan, s, flight[s], vectors.shape[0])
            ready = joined(own, shift(flip, "core", 1))
            parts += [ready[0]] + [shift(ready[k], ORDERS[s][2], k) for k in range(1, RING)]
        return final(inner, parts)

    first = staged(0, state)
    second = staged(1, first)
    return lax.cond(plan[5 * STREAMS, 0] > 0, all_dense, lambda: (first, second))


def solution(mesh):
    split = P(AXES)
    return jax.shard_map(
        shards,
        mesh=mesh,
        in_specs=(split,) * 8 + (P(),),
        out_specs=(split, split),
        check_vma=False,
    )
```

```python
import functools

import jax
import jax.numpy as jnp
from jax import lax
from jax.experimental import pallas as pl
from jax.experimental.pallas import tpu as pltpu
from jax.sharding import PartitionSpec as P
import numpy as np

AXES = ("body", "blk")
ANY = pl.BlockSpec(memory_space=pl.ANY)
VMEM = pl.BlockSpec(memory_space=pltpu.VMEM)
SMEM = pl.BlockSpec(memory_space=pltpu.SMEM)
LIMIT = 40 * 1024 * 1024


def near_core(shape, kind):
    return pltpu.VMEM(shape, kind)


def pinned(values):
    return [pltpu.with_memory_space_constraint(v, pltpu.VMEM) for v in values]


GROUP = 4
SLOTS = 128
STREAMS, RING = 3, 4
REACH, CELL, NEAR, PHASES = 32, 8, 12, 4
FIRST, SECOND = 23, 25
ROWS = ((0, 112), (112, 112), (224, 96))
ORDERS = (("z", "y", "x"), ("y", "x", "z"), ("x", "z", "y"))


def dot(a, b):
    return jnp.dot(a, b, preferred_element_type=jnp.float32)


def product_kernel(source, slot, near, vectors, diag, nbr, donor, out, inner,
                   donor_buf, diag_buf, nbr_buf, made, donor_sem, diag_sem, nbr_sem, out_sem):
    count = donor.shape[0]
    blocks, fan = nbr.shape[0], nbr.shape[1]

    def donor_copy(g):
        part = pl.ds(g * GROUP, GROUP)
        return pltpu.make_async_copy(donor.at[part], donor_buf.at[part], donor_sem.at[g])

    def nbr_copy(b):
        return pltpu.make_async_copy(nbr.at[b], nbr_buf.at[b], nbr_sem.at[b])

    def out_copy(e):
        return pltpu.make_async_copy(made.at[e], out.at[slot[e]], out_sem.at[e])

    diag_copy = pltpu.make_async_copy(diag, diag_buf, diag_sem)
    for g in range(count // GROUP):
        donor_copy(g).start()
    diag_copy.start()
    for b in range(blocks):
        nbr_copy(b).start()

    @pl.loop(0, count // GROUP)
    def _(g):
        donor_copy(g).wait()
        for i in range(GROUP):
            e = g * GROUP + i
            made[e] = dot(donor_buf[e], vectors[source[e]]).astype(made.dtype)
            out_copy(e).start()

    diag_copy.wait()

    @pl.loop(0, blocks)
    def _(b):
        nbr_copy(b).wait()
        total = dot(diag_buf[b], vectors[b])
        for k in range(fan):
            total = total + dot(nbr_buf[b, k], vectors[near[b * fan + k]])
        inner[b] = total

    @pl.loop(0, count)
    def _(e):
        out_copy(e).wait()


def products(source, slot, near, vectors, diag, nbr, donor, slots):
    count = donor.shape[0]
    blocks, width, columns = vectors.shape
    return pl.pallas_call(
        product_kernel,
        out_shape=(
            jax.ShapeDtypeStruct((slots, width, columns), vectors.dtype),
            jax.ShapeDtypeStruct((blocks, width, columns), jnp.float32),
        ),
        in_specs=[SMEM, SMEM, SMEM, VMEM, ANY, ANY, ANY],
        out_specs=(ANY, VMEM),
        scratch_shapes=[
            pltpu.VMEM(donor.shape, donor.dtype),
            pltpu.VMEM(diag.shape, diag.dtype),
            pltpu.VMEM(nbr.shape, nbr.dtype),
            pltpu.VMEM((count, width, columns), vectors.dtype),
            pltpu.SemaphoreType.DMA((count // GROUP,)),
            pltpu.SemaphoreType.DMA,
            pltpu.SemaphoreType.DMA((blocks,)),
            pltpu.SemaphoreType.DMA((count,)),
        ],
        compiler_params=pltpu.CompilerParams(vmem_limit_bytes=LIMIT),
        name="products",
    )(source, slot, near, vectors, diag, nbr, donor)


def sum_kernel(target, inner, incoming, out, buf, total, sem):
    slots = incoming.shape[0]

    def copy(s):
        return pltpu.make_async_copy(incoming.at[s], buf.at[s], sem.at[s])

    @pl.loop(0, slots)
    def _(s):
        @pl.when(target[s] >= 0)
        def _():
            copy(s).start()

    total[...] = inner[...]

    @pl.loop(0, slots)
    def _(s):
        @pl.when(target[s] >= 0)
        def _():
            copy(s).wait()
            r = target[s]
            total[r] = total[r] + buf[s].astype(jnp.float32)

    out[...] = total[...].astype(out.dtype)


def summed(target, inner, incoming):
    return pl.pallas_call(
        sum_kernel,
        out_shape=jax.ShapeDtypeStruct(inner.shape, incoming.dtype),
        in_specs=[SMEM, VMEM, ANY],
        out_specs=VMEM,
        scratch_shapes=[
            pltpu.VMEM(incoming.shape, incoming.dtype),
            pltpu.VMEM(inner.shape, jnp.float32),
            pltpu.SemaphoreType.DMA((incoming.shape[0],)),
        ],
        compiler_params=pltpu.CompilerParams(vmem_limit_bytes=LIMIT),
        name="summed",
    )(target, inner, incoming)

def inner_kernel(near, vectors, diag, nbr, inner, diag_buf, nbr_buf, diag_sem, nbr_sem):
    blocks, fan = nbr.shape[0], nbr.shape[1]

    def nbr_copy(b):
        return pltpu.make_async_copy(nbr.at[b], nbr_buf.at[b], nbr_sem.at[b])

    diag_copy = pltpu.make_async_copy(diag, diag_buf, diag_sem)
    diag_copy.start()
    for b in range(blocks):
        nbr_copy(b).start()
    diag_copy.wait()

    @pl.loop(0, blocks)
    def _(b):
        nbr_copy(b).wait()
        total = dot(diag_buf[b], vectors[b])
        for k in range(fan):
            total = total + dot(nbr_buf[b, k], vectors[near[b * fan + k]])
        inner[b] = total


def interior(near, vectors, diag, nbr):
    blocks, width, columns = vectors.shape
    return pl.pallas_call(
        inner_kernel,
        out_shape=near_core((blocks, width, columns), jnp.float32),
        in_specs=[SMEM, VMEM, ANY, ANY],
        out_specs=VMEM,
        scratch_shapes=[
            pltpu.VMEM(diag.shape, diag.dtype),
            pltpu.VMEM(nbr.shape, nbr.dtype),
            pltpu.SemaphoreType.DMA,
            pltpu.SemaphoreType.DMA((blocks,)),
        ],
        compiler_params=pltpu.CompilerParams(vmem_limit_bytes=18 * 2**20),
        cost_estimate=pl.CostEstimate(flops=4 * 10**9, bytes_accessed=2 * 10**7, transcendentals=0),
        name="interior",
    )(near, vectors, diag, nbr)


def donate_kernel(turn, phase, source, table, vectors, donor, target, *refs):
    outs, refs = refs[:STREAMS * RING], refs[STREAMS * RING:]
    spread, refs = refs[0], refs[1:]
    spread[...] = jnp.broadcast_to(target[pl.ds(2 * STREAMS, 1)][None], spread.shape)
    donor_buf, made, donor_sem = refs
    count = donor.shape[0]

    def donor_copy(g):
        part = pl.ds(g * GROUP, GROUP)
        return pltpu.make_async_copy(donor.at[part], donor_buf.at[part], donor_sem.at[g])

    for g in range(count // GROUP):
        donor_copy(g).start()

    @pl.loop(0, count // GROUP)
    def _(g):
        donor_copy(g).wait()
        for i in range(GROUP):
            e = g * GROUP + i
            made[e] = dot(donor_buf[e], vectors[source[e * PHASES + phase[turn]]]).astype(made.dtype)

    for s, (start, rows) in enumerate(ROWS):
        for k in range(RING):
            out = outs[s * RING + k]
            @pl.loop(0, jnp.minimum(table[STREAMS + s, k], FIRST))
            def _(j, out=out, s=s, k=k, start=start, rows=rows):
                out[j] = made[table[s, k * REACH + j], pl.ds(start, rows)]


def donate(turn, phase, source, table, vectors, donor):
    count = donor.shape[0]
    width, columns = vectors.shape[1:]
    shapes = [(rows, columns) for _, rows in ROWS for _ in range(RING)]
    return pl.pallas_call(
        functools.partial(donate_kernel, turn),
        out_shape=tuple(near_core((FIRST,) + s, vectors.dtype) for s in shapes)
        + (near_core((SLOTS, 1, SLOTS), jnp.int32),),
        in_specs=[SMEM, SMEM, SMEM, VMEM, ANY, VMEM],
        out_specs=(VMEM,) * (len(shapes) + 1),
        scratch_shapes=[
            pltpu.VMEM(donor.shape, donor.dtype),
            pltpu.VMEM((count, width, columns), vectors.dtype),
            pltpu.SemaphoreType.DMA((count // GROUP,)),
        ],
        compiler_params=pltpu.CompilerParams(vmem_limit_bytes=28 * 2**20),
        name="donate",
    )(phase, source, table, vectors, donor, table)


def relay_kernel(row, table, *refs):
    ins, outs = refs[:RING], refs[RING:]
    held = [jnp.int32(0)] * RING
    for i in range(RING):
        taken = jnp.int32(0)
        for k in range(RING):
            count = table[STREAMS + row, i * RING + k]

            @pl.loop(0, jnp.minimum(count, jnp.minimum(FIRST - taken, SECOND - held[k])))
            def _(j, i=i, k=k, into=held[k], out_of=taken):
                outs[k][into + j] = ins[i][out_of + j]

            held[k], taken = held[k] + count, taken + count


def relay(table, row, ins):
    shape, kind = ins[0].shape[1:], ins[0].dtype
    return pl.pallas_call(
        functools.partial(relay_kernel, row),
        out_shape=(near_core((SECOND,) + shape, kind),) * RING,
        in_specs=[SMEM] + [VMEM] * RING,
        out_specs=(VMEM,) * RING,
        compiler_params=pltpu.CompilerParams(vmem_limit_bytes=8 * 2**20),
        cost_estimate=pl.CostEstimate(flops=10**6, bytes_accessed=6 * 10**6, transcendentals=0),
        name="relay",
    )(table, *pinned(ins))


def gather_kernel(row, table, *refs):
    ins, (own, flip, total) = refs[:RING], refs[RING:]
    blocks = own.shape[0] // RING

    @pl.loop(0, 2 * RING * blocks, unroll=2)
    def _(cell):
        total[cell] = jnp.zeros(total.shape[1:], total.dtype)

    for i in range(RING):

        @pl.loop(0, jnp.minimum(table[2 * STREAMS + row, i], SECOND))
        def _(j, i=i):
            cell = table[row, i * REACH + j]
            total[cell] = total[cell] + ins[i][j].astype(jnp.float32)

    @pl.loop(0, RING * blocks, unroll=2)
    def _(cell):
        own[cell] = total[cell].astype(own.dtype)
        flip[cell] = total[RING * blocks + cell].astype(flip.dtype)


def gathered(table, row, ins, blocks):
    shape, kind = ins[0].shape[1:], ins[0].dtype
    return pl.pallas_call(
        functools.partial(gather_kernel, row),
        out_shape=(
            near_core((RING * blocks,) + shape, kind),
            near_core((RING * blocks,) + shape, kind),
        ),
        in_specs=[SMEM] + [VMEM] * RING,
        out_specs=(VMEM, VMEM),
        scratch_shapes=[pltpu.VMEM((2 * RING * blocks,) + shape, jnp.float32)],
        compiler_params=pltpu.CompilerParams(vmem_limit_bytes=12 * 2**20),
        cost_estimate=pl.CostEstimate(flops=10**6, bytes_accessed=6 * 10**6, transcendentals=0),
        name="gathered",
    )(table, *pinned(ins))


def join_kernel(own, flip, *outs):
    blocks = outs[0].shape[0]

    @pl.loop(0, blocks)
    def _(b):
        for k in range(RING):
            both = own[k * blocks + b].astype(jnp.float32) + flip[k * blocks + b].astype(jnp.float32)
            outs[k][b] = both.astype(outs[k].dtype)


def joined(own, flip):
    blocks = own.shape[0] // RING
    return pl.pallas_call(
        join_kernel,
        out_shape=(near_core((blocks,) + own.shape[1:], flip.dtype),) * RING,
        in_specs=[VMEM, VMEM],
        out_specs=(VMEM,) * RING,
        compiler_params=pltpu.CompilerParams(vmem_limit_bytes=8 * 2**20),
        cost_estimate=pl.CostEstimate(flops=10**6, bytes_accessed=5 * 10**6, transcendentals=0),
        name="joined",
    )(*pinned((own, flip)))


def final_kernel(inner, *refs):
    parts, out = refs[:-1], refs[-1]

    @pl.loop(0, out.shape[0])
    def _(b):
        for s, (start, rows) in enumerate(ROWS):
            part = pl.ds(start, rows)
            total = inner[b, part]
            for k in range(RING):
                total = total + parts[s * RING + k][b].astype(jnp.float32)
            out[b, part] = total.astype(out.dtype)


def final(inner, parts):
    return pl.pallas_call(
        final_kernel,
        out_shape=jax.ShapeDtypeStruct(inner.shape, parts[0].dtype),
        in_specs=[VMEM] * (1 + len(parts)),
        out_specs=VMEM,
        compiler_params=pltpu.CompilerParams(vmem_limit_bytes=12 * 2**20),
        name="final",
    )(*pinned((inner, *parts)))


def place(index):
    return {"z": index // 32, "core": index // 16 % 2, "y": index // 4 % 4, "x": index % 4}


def number(at):
    return ((at["z"] * 2 + at["core"]) * 4 + at["y"]) * 4 + at["x"]


def shift(value, axis, step):
    if axis in ("z", "core"):
        name, size = "body", 8
        move = (lambda i: (i + 2 * step) % 8) if axis == "z" else (lambda i: i ^ 1)
    else:
        name, size = "blk", 16
        if axis == "y":
            move = lambda i: (i + 4 * step) % 16
        else:
            move = lambda i: i // 4 * 4 + (i + step) % 4
    return lax.ppermute(value, name, [(i, move(i)) for i in range(size)])


def offsets(order):
    grid = np.meshgrid(*[np.arange(2 if n == "f" else 4) for n in order], indexing="ij")
    return {n: g.reshape(-1) for n, g in zip(order, grid)}


def spots(stage):
    senders, takers = [], []
    for one, two, three in ORDERS:
        o = offsets(("2", "1", "f", "3") if stage == 3 else ("1", "2", "f", "3"))
        sender = {n: np.zeros(SLOTS, np.int64) for n in ("z", "core", "y", "x")}
        taker = {n: np.zeros(SLOTS, np.int64) for n in ("z", "core", "y", "x")}
        if stage == 1:
            taker[one] = o["1"]
        else:
            sender[one] = -o["1"] % 4
        if stage == 3:
            sender[two] = -o["2"] % 4
        else:
            taker[two] = o["2"]
        taker["core"], taker[three] = o["f"], o["3"]
        senders.append(number(sender))
        takers.append(number(taker))
    return np.concatenate(senders).astype(np.int32), np.concatenate(takers).astype(np.int32)


def moved(here, step):
    me, step = place(here), place(step)
    return number({n: (me[n] ^ step[n]) if n == "core" else (me[n] + step[n]) % 4 for n in me})


def mover(here):
    def spread(index):
        return index >> 5, (index >> 4) & 1, (index >> 2) & 3, index & 3

    def move(step):
        mine, step = spread(here), spread(step)
        z, y, x = ((mine[i] + step[i]) & 3 for i in (0, 2, 3))
        return ((z * 2 + (mine[1] ^ step[1])) * 4 + y) * 4 + x

    return move


def ones(mask):
    return jnp.where(mask, 1.0, 0.0).astype(jnp.bfloat16)


def rows_of(flat):
    return [flat[:, i * SLOTS:(i + 1) * SLOTS] for i in range(flat.shape[1] // SLOTS)]


def folded(rows):
    down = lax.broadcasted_iota(jnp.int32, (SLOTS, SLOTS), 0)
    across = lax.broadcasted_iota(jnp.int32, (SLOTS, SLOTS), 1)
    lane = lax.broadcasted_iota(jnp.int32, (1, SLOTS), 1)
    before = ones((down < across) & (down // REACH == across // REACH))
    lists, counts = [], []
    for value in rows:
        real = value >= 0.0
        valid = jnp.broadcast_to(ones(real), (8, SLOTS))
        rank = dot(valid, before)[:1].astype(jnp.int32)
        spot = jnp.where(real, (lane & -REACH) + rank, -1)
        value = jnp.broadcast_to(value.astype(jnp.bfloat16), (8, SLOTS))
        lists.append(lax.dot_general(
            value, ones(down == spot), (((1,), (1,)), ((), ())), preferred_element_type=jnp.float32
        )[:1])
        counts.append(dot(valid, ones(down // REACH == across))[:1])
    return lists, counts


def choice_kernel(here, slot, recv, wanted, out):
    count = slot.shape[1]
    shape = (SLOTS, count)
    hit = lax.broadcasted_iota(jnp.int32, shape, 0) == slot[...]
    tile = lax.broadcasted_iota(jnp.int32, shape, 1).astype(jnp.float32) + 1.0
    tile = jnp.max(jnp.where(hit, tile, 0.0), axis=1, keepdims=True)
    ids = lax.broadcasted_iota(jnp.int32, (SLOTS, wanted.shape[1]), 0)
    chosen = jnp.where(ids == mover(here[0])(wanted[...]), tile, 0.0)
    chosen = jnp.sum(chosen, axis=0, keepdims=True) - 1.0
    target = jnp.broadcast_to((recv[...].astype(jnp.float32) + 1.0).astype(jnp.bfloat16), (8, count))
    target = lax.dot_general(
        target, ones(hit), (((1,), (1,)), ((), ())), preferred_element_type=jnp.float32
    )[:1] - 1.0
    lists, counts = folded(rows_of(chosen))
    for row, value in enumerate(lists + counts + [target]):
        out[pl.ds(row, 1)] = value.astype(jnp.int32)


def choices(here, slot, recv):
    return pl.pallas_call(
        choice_kernel,
        out_shape=jax.ShapeDtypeStruct((8, SLOTS), jnp.int32),
        in_specs=[SMEM] + [VMEM] * 3,
        out_specs=VMEM,
        compiler_params=pltpu.CompilerParams(vmem_limit_bytes=12 * 2**20),
        name="choices",
    )(here.reshape(1), slot.reshape(1, -1), recv.reshape(1, -1), jnp.asarray(spots(1)[1][None, :]))


def table_kernel(here, pattern, senders, takers, firsts, lefts, rights, same, out):
    move = mover(here[0])
    whole = pattern[...].astype(jnp.float32)
    ids = lax.broadcasted_iota(jnp.int32, (SLOTS, senders.shape[1]), 0)
    picked = lax.dot_general(
        (whole + 1.0).astype(jnp.bfloat16), ones(ids == move(senders[...])), (((0,), (0,)), ((), ())),
        preferred_element_type=jnp.float32,
    )
    picked = jnp.sum(jnp.where(ids == move(takers[...]), picked, 0.0), axis=0, keepdims=True) - 1.0
    picked = rows_of(picked)
    lane = lax.broadcasted_iota(jnp.int32, (1, SLOTS), 1)
    cell = (((lane >> 2) & 1) * (RING * NEAR) + (lane & 3) * NEAR).astype(jnp.float32)
    lists, counts = folded([jnp.where(r >= 0.0, r + cell, -1.0) for r in picked[STREAMS:]])
    down = lax.broadcasted_iota(jnp.int32, (SLOTS, SLOTS), 0)
    across = lax.broadcasted_iota(jnp.int32, (SLOTS, SLOTS), 1)
    runs = [
        dot(jnp.broadcast_to(ones(r >= 0.0), (8, SLOTS)), ones(down // CELL == across))[:1]
        for r in picked[:STREAMS]
    ]
    real = ones(whole >= 0.0)
    one = jnp.max(dot(real, firsts[...]), keepdims=True) - FIRST
    two = dot(dot(lefts[...], real).astype(jnp.bfloat16), rights[...]) * same[...]
    over = jnp.maximum(one, jnp.max(two, keepdims=True) - SECOND)
    for row, value in enumerate(lists + runs + counts + [jnp.broadcast_to(over, (1, SLOTS))]):
        out[pl.ds(row, 1)] = value.astype(jnp.int32)


def tables(here, pattern):
    senders, takers = (np.concatenate(pair)[None, :] for pair in zip(spots(2), spots(3)))
    at = place(np.arange(SLOTS))
    firsts, lefts, rights = [], [], []
    for one, two, three in ORDERS:
        firsts.append(np.arange(4)[None, :] == at[one][:, None])
        lefts.append(np.arange(32)[:, None] == ((at["core"] * 4 + at[two]) * 4 + at[three])[None, :])
        rights.append(np.arange(16)[None, :] == (at[one] * 4 + at[two])[:, None])
    same = (np.arange(STREAMS * 32) // 32)[:, None] == (np.arange(STREAMS * 16) // 16)[None, :]
    return pl.pallas_call(
        table_kernel,
        out_shape=jax.ShapeDtypeStruct((16, SLOTS), jnp.int32),
        in_specs=[SMEM] + [VMEM] * 7,
        out_specs=VMEM,
        compiler_params=pltpu.CompilerParams(vmem_limit_bytes=12 * 2**20),
        name="tables",
    )(
        here.reshape(1),
        pattern,
        jnp.asarray(senders),
        jnp.asarray(takers),
        jnp.asarray(np.concatenate(firsts, 1), jnp.bfloat16),
        jnp.asarray(np.concatenate(lefts, 0), jnp.bfloat16),
        jnp.asarray(np.concatenate(rights, 1), jnp.bfloat16),
        jnp.asarray(same, jnp.float32),
    )


def shards(state, diag, nbr, near, donor, donor_src, donor_slot, donor_recv, phase):
    here = lax.axis_index("body") * lax.axis_size("blk") + lax.axis_index("blk")
    flat = near.reshape(-1), donor_src.reshape(-1)
    near_flat, by_phase, state, donor_slot = lax.optimization_barrier((*flat, state, donor_slot))
    chosen = choices(here, donor_slot, donor_recv)

    def dense(vectors, column):
        pattern = held[1]
        source = lax.dynamic_slice_in_dim(donor_src, column, 1, axis=1)[:, 0]
        target = lax.dynamic_slice_in_dim(pattern, here, 1, axis=1)[:, 0]
        outgoing, inner = products(source, donor_slot, near_flat, vectors, diag, nbr, donor, SLOTS)
        incoming = lax.all_to_all(outgoing, AXES, split_axis=0, concat_axis=0, tiled=True)
        out = summed(target, inner, incoming)
        return out, out

    def all_dense():
        return tuple(lax.scan(dense, state, phase)[1])

    def staged(turn, vectors, plan):
        *sent, spread = donate(turn, phase, by_phase, chosen, vectors, donor)
        if plan is None:
            pattern = lax.all_to_all(spread, AXES, split_axis=0, concat_axis=0, tiled=True)[:, 0]
            plan = tables(here, pattern), pattern
        inner = interior(near_flat, vectors, diag, nbr)
        parts = []
        inner, tied = lax.optimization_barrier((inner, plan[0]))
        flight = [
            [sent[s * RING]] + [shift(sent[s * RING + k], ORDERS[s][0], k) for k in range(1, RING)]
            for s in range(STREAMS)
        ]
        passed = [relay(tied, s, flight[s]) for s in range(STREAMS)]
        flight = [
            [passed[s][0]] + [shift(passed[s][k], ORDERS[s][1], k) for k in range(1, RING)]
            for s in range(STREAMS)
        ]
        for s in range(STREAMS):
            own, flip = gathered(tied, s, flight[s], vectors.shape[0])
            ready = joined(own, shift(flip, "core", 1))
            parts += [ready[0]] + [shift(ready[k], ORDERS[s][2], k) for k in range(1, RING)]
        return final(inner, parts), plan

    first, held = staged(0, state, None)
    second, _ = staged(1, first, held)
    return lax.cond(held[0][3 * STREAMS, 0] > 0, all_dense, lambda: (first, second))


def solution(mesh):
    split = P(AXES)
    return jax.shard_map(
        shards,
        mesh=mesh,
        in_specs=(split,) * 8 + (P(),),
        out_specs=(split, split),
        check_vma=False,
    )
```
